32 devices in a mesh: lat: 4 (over y, x), lon: 8 (over z, core).
Axes of the slice: x: 2, y: 2, z: 4, core: 2. Of those that a mesh axis runs over, the one named last changes fastest.
Arguments:
- field: bfloat16 [128, 256, 512], P('lat', 'lon'), may hold values from -6 to 6
- qkv_fine: bfloat16 [512, 1536], replicated, may hold values from -0.35355339 to 0.35355339
- proj_fine: bfloat16 [512, 512], replicated, may hold values from -0.25 to 0.25
- up_fine: bfloat16 [512, 2048], replicated, may hold values from -0.25 to 0.25
- down_fine: bfloat16 [2048, 512], replicated, may hold values from -0.125 to 0.125
- merge_weight: bfloat16 [2048, 1024], replicated, may hold values from -0.15467961 to 0.15467961
- qkv_coarse: bfloat16 [1024, 3072], P(None, 'lon'), may hold values from -0.25 to 0.25
- proj_coarse: bfloat16 [1024, 1024], P(None, 'lon'), may hold values from -0.1875 to 0.1875
Outputs:
- fine_out: bfloat16 [128, 256, 512], P('lat', 'lon')
- coarse_out: bfloat16 [64, 128, 1024], P('lat', 'lon')
The draws below stay inside these ranges and needn't reach their ends.
All inputs are finite; a program needn't handle non-finite values.
Results may differ from the reference program's by a relative error of at most 0.018.
Values may be sent and summed in bfloat16 or wider, within the bound.
No kernel may reach another device: no remote copies, remote signals or barrier semaphores. Data moves between devices by JAX's collectives and lax.ppermute only.
A program may use at most 128 MiB of HBM per device.

```python
import jax
import jax.numpy as jnp
from jax import lax

C1 = 512
C2 = 1024
HID1 = 2048
HEAD = 64
WIN = 16
H1 = 128
W1 = 256


def draw_field(key, part):
    noise_key = jax.random.fold_in(jax.random.fold_in(key, 101), 0)
    noise = jnp.clip(jax.random.normal(noise_key, (H1, W1, C1), jnp.float32), -6.0, 6.0)
    return noise.astype(jnp.bfloat16)


def draw_qkv_fine(key, part):
    base = jnp.clip(jax.random.normal(jax.random.fold_in(key, 202), (C1, 3 * C1), jnp.float32), -6.0, 6.0)
    base = base * C1 ** (-0.5)
    return base.astype(jnp.bfloat16)


def draw_merge_weight(key, part):
    base = jnp.clip(jax.random.normal(jax.random.fold_in(key, 303), (4 * C1, C2), jnp.float32), -6.0, 6.0)
    base = base * (4 * C1) ** (-0.5)
    return base.astype(jnp.bfloat16)


def draw_qkv_coarse(key, part):
    base = jnp.clip(jax.random.normal(jax.random.fold_in(key, 404), (C2, 3 * C2), jnp.float32), -6.0, 6.0)
    base = base * C2 ** (-0.5)
    return base.astype(jnp.bfloat16)


def steps_of(own_key, shape, cuts, least, largest):
    def one(axis_at, parts):
        steps = jax.random.uniform(jax.random.fold_in(jax.random.fold_in(own_key, 6), axis_at), (parts,), jnp.float32, least / len(cuts), largest / len(cuts))
        return jnp.repeat(jnp.exp(steps), shape[axis_at] // parts).reshape((-1,) + (1,) * (len(shape) - axis_at - 1))

    loudness = one(*cuts[0])
    for cut in cuts[1:]:
        loudness = loudness * one(*cut)
    return loudness


def centred(rng, shape, scale, most, shards=(), kind=jnp.bfloat16):
    values = jax.random.normal(rng, shape, jnp.float32) * scale
    if len(shards) > 0:
        values = steps_of(rng, shape, shards, -0.22, 0.18) * values
    return jnp.clip(values, min=-most, max=most).astype(kind)


def setup_inputs(seed: int = 0) -> dict:
    key_of = jax.random.split(jax.random.key(seed), 9)
    field = draw_field(jax.random.fold_in(key_of[8], 71), 0)
    qkv_fine = draw_qkv_fine(jax.random.fold_in(key_of[8], 71), 0)
    proj_fine = centred(key_of[2], (C1, C1), C1 ** -0.5, 0.25)
    up_fine = centred(key_of[3], (C1, HID1), C1 ** -0.5, 0.25)
    down_fine = centred(key_of[4], (HID1, C1), HID1 ** -0.5, 0.125)
    merge_weight = draw_merge_weight(jax.random.fold_in(key_of[8], 71), 0)
    qkv_coarse = draw_qkv_coarse(jax.random.fold_in(key_of[8], 71), 0)
    proj_coarse = centred(key_of[7], (C2, C2), C2 ** -0.5, 0.1875, ((1, 8),))
    return dict(field=field, qkv_fine=qkv_fine, proj_fine=proj_fine, up_fine=up_fine, down_fine=down_fine, merge_weight=merge_weight, qkv_coarse=qkv_coarse, proj_coarse=proj_coarse)


def normalize(values):
    values = values.astype(jnp.float32)
    center = values - lax.optimization_barrier(jnp.mean(values, axis=-1, keepdims=True))
    spread = lax.optimization_barrier(jnp.mean(center * center, axis=-1, keepdims=True))
    return center * lax.rsqrt(spread + 1e-05)

def window_core(qkv, label):
    cols_total = qkv.shape[1]
    width = qkv.shape[2] // 3
    heads = width // HEAD
    blocks = cols_total // WIN
    packed = qkv.reshape(WIN, blocks, WIN, 3, heads, HEAD).transpose(3, 1, 4, 0, 2, 5)
    packed = packed.reshape(3, blocks, heads, WIN * WIN, HEAD).astype(jnp.float32)
    scores = jnp.einsum('nhqd,nhkd->nhqk', packed[0], packed[1]) * HEAD ** (-0.5)
    tags = jnp.repeat(label, WIN)
    allowed = tags[:, None] == tags[None, :]
    scores = jnp.where(allowed, scores, -1e+30)
    weights = jax.nn.softmax(scores, axis=-1).astype(jnp.bfloat16)
    mixed = jnp.einsum('nhqk,nhkd->nhqd', weights.astype(jnp.float32), packed[2]).astype(jnp.bfloat16)
    mixed = mixed.reshape(blocks, heads, WIN, WIN, HEAD).transpose(2, 0, 3, 1, 4)
    return mixed.reshape(WIN, cols_total, width)

def shifted_mix(values, w_qkv):
    rows_total, cols_total, width = values.shape
    half_win = WIN // 2
    rolled = jnp.roll(values, (-half_win, -half_win), (0, 1))
    anchor = (jnp.arange(rows_total, dtype=jnp.int32) + half_win) % rows_total
    label = (anchor < half_win).astype(jnp.int32).reshape(rows_total // WIN, WIN)

    def one_strip(pair):
        strip, tags = pair
        normed = normalize(strip).astype(jnp.bfloat16).reshape(-1, width)
        qkv = jnp.dot(normed, w_qkv, preferred_element_type=jnp.float32).astype(jnp.bfloat16)
        return window_core(qkv.reshape(WIN, cols_total, 3 * width), tags)
    mixed = lax.map(one_strip, (rolled.reshape(rows_total // WIN, WIN, cols_total, width), label))
    mixed = mixed.reshape(rows_total, cols_total, width)
    return jnp.roll(mixed, (half_win, half_win), (0, 1))

def reference(field, qkv_fine, proj_fine, up_fine, down_fine, merge_weight, qkv_coarse, proj_coarse):
    rows_total, cols_total, width = field.shape
    mixed = shifted_mix(field, qkv_fine)

    def finish(pair):
        strip, part = pair
        attend = jnp.dot(part.reshape(-1, width), proj_fine, preferred_element_type=jnp.float32)
        attended = (strip.reshape(-1, width).astype(jnp.float32) + attend).astype(jnp.bfloat16)
        normed = normalize(attended).astype(jnp.bfloat16)
        hidden = jax.nn.gelu(jnp.dot(normed, up_fine, preferred_element_type=jnp.float32)).astype(jnp.bfloat16)
        output = attended.astype(jnp.float32) + jnp.dot(hidden, down_fine, preferred_element_type=jnp.float32)
        return output.astype(jnp.bfloat16).reshape(WIN, cols_total, width)
    strips = rows_total // WIN
    fine_out = lax.map(finish, (field.reshape(strips, WIN, cols_total, width), mixed.reshape(strips, WIN, cols_total, width)))
    fine_out = fine_out.reshape(rows_total, cols_total, width)
    joined = fine_out.reshape(rows_total // 2, 2, cols_total // 2, 2, width).transpose(0, 2, 3, 1, 4)
    joined = joined.reshape(-1, 4 * width)
    merged = jnp.dot(normalize(joined).astype(jnp.bfloat16), merge_weight, preferred_element_type=jnp.float32)
    wide = merge_weight.shape[1]
    merged = merged.astype(jnp.bfloat16).reshape(rows_total // 2, cols_total // 2, wide)
    coarse_mix = shifted_mix(merged, qkv_coarse)
    attend = jnp.dot(coarse_mix.reshape(-1, wide), proj_coarse, preferred_element_type=jnp.float32)
    coarse_out = (merged.reshape(-1, wide).astype(jnp.float32) + attend).astype(jnp.bfloat16)
    return (fine_out, coarse_out.reshape(rows_total // 2, cols_total // 2, wide))
```

```python
import functools

import jax
import jax.numpy as jnp
import numpy as np
from jax import lax
from jax.experimental import pallas as pl
from jax.experimental.pallas import tpu as pltpu
from jax.sharding import PartitionSpec as P

HEAD = 64
WIN = 16
HALF = WIN // 2
QUART = HALF // 2
TOK = WIN * WIN
SLAB = 2 * HEAD
NEG = -1e30
BF = jnp.bfloat16
F32 = jnp.float32


def dot(a, b):
    return jnp.dot(a, b, preferred_element_type=F32)


def norm(values):
    center = values - jnp.mean(values, axis=-1, keepdims=True)
    spread = jnp.mean(center * center, axis=-1, keepdims=True)
    return (center * lax.rsqrt(spread + 1e-05)).astype(BF)


def slab_attention(qkv, mixed, at, width, bias):
    q = qkv[:, pl.ds(at, SLAB)] * BF(HEAD ** (-0.5))
    k = qkv[:, pl.ds(at + width, SLAB)]
    v = qkv[:, pl.ds(at + 2 * width, SLAB)]
    low = lax.broadcasted_iota(jnp.int32, (TOK, SLAB), 1) < HEAD
    zero = jnp.zeros_like(q)
    one = jnp.ones_like(v)
    outs = []
    for qh, vh in (
        (jnp.where(low, q, zero), jnp.where(low, v, one)),
        (jnp.where(low, zero, q), jnp.where(low, one, v)),
    ):
        scores = lax.dot_general(qh, k, (((1,), (1,)), ((), ())), preferred_element_type=F32)
        if bias is not None:
            scores = scores + bias
        top = jnp.max(scores, axis=-1, keepdims=True)
        outs.append(dot(jnp.exp(scores - top).astype(BF), vh))
    sums = pltpu.roll(jnp.where(low, outs[1], outs[0]), HEAD, 1)
    mixed[:, pl.ds(at, SLAB)] = (jnp.where(low, outs[0], outs[1]) / sums).astype(BF)


def attention(qkv, mixed, width, bias):
    def step(j, carry):
        slab_attention(qkv, mixed, pl.multiple_of(j * SLAB, SLAB), width, bias)
        return carry

    lax.fori_loop(0, width // SLAB, step, 0)


def mask_bias(last_ref):
    lead = lax.broadcasted_iota(jnp.int32, (TOK, TOK), 0) < TOK // 2
    other = lax.broadcasted_iota(jnp.int32, (TOK, TOK), 1) < TOK // 2
    return jnp.where(lead == other, 0.0, jnp.where(last_ref[0] > 0, NEG, 0.0))


def fine_kernel(masked, last, x_ref, wq, wp, wu, wd, wm, out_ref, merged_ref,
                vq, vp, vu, vd, vm, qkv, mixed, wide, sems):
    pairs = ((wq, vq), (wp, vp), (wu, vu), (wd, vd), (wm, vm))
    copies = [pltpu.make_async_copy(src, dst, sems.at[i]) for i, (src, dst) in enumerate(pairs)]
    for copy in copies:
        copy.start()
    width = x_ref.shape[1]
    x = x_ref[...].astype(F32)
    normed = norm(x)
    copies[0].wait()
    for part in range(3):
        cols = slice(part * width, (part + 1) * width)
        qkv[:, cols] = dot(normed, vq[:, cols]).astype(BF)
    attention(qkv, mixed, width, mask_bias(last) if masked else None)
    copies[1].wait()
    attended = (x + dot(mixed[...], vp[...])).astype(BF).astype(F32)
    normed = norm(attended)
    copies[2].wait()
    copies[3].wait()
    total = attended
    step = width
    for at in range(0, vu.shape[1], step):
        hidden = jax.nn.gelu(dot(normed, vu[:, at:at + step])).astype(BF)
        total = total + dot(hidden, vd[at:at + step, :])
    fine = total.astype(BF)
    out_ref[...] = fine
    for c in range(width // 128):
        wide[c] = fine[:, c * 128:(c + 1) * 128].astype(F32)
    groups = []
    for b in range(2):
        picked = jnp.concatenate(
            [wide[c, pl.ds(b, TOK // 2, stride=2), :] for c in range(width // 128)], axis=1
        ).reshape(HALF, 2, HALF, width)
        groups.append((picked[:, 0].reshape(TOK // 4, width), picked[:, 1].reshape(TOK // 4, width)))
    joined = [groups[0][0], groups[0][1], groups[1][0], groups[1][1]]
    count = 4 * width
    mean = sum(jnp.sum(g, axis=-1, keepdims=True) for g in joined) / count
    joined = [g - mean for g in joined]
    spread = sum(jnp.sum(g * g, axis=-1, keepdims=True) for g in joined) / count
    scale = lax.rsqrt(spread + 1e-05)
    copies[4].wait()
    merged = 0.0
    for i, g in enumerate(joined):
        merged = merged + dot((g * scale).astype(BF), vm[i * width:(i + 1) * width, :])
    merged_ref[...] = merged.astype(BF)


def fine_window(x, last, weights, masked):
    width = x.shape[-1]
    wide = weights[-1].shape[1]
    flops = 2 * TOK * width * (3 * width + width + 4 * width * 2) + TOK * 2 * width * wide
    size = sum(w.size * 2 for w in weights)
    hbm = pl.BlockSpec(memory_space=pl.ANY)
    vmem = pl.BlockSpec(memory_space=pltpu.VMEM)
    return pl.pallas_call(
        functools.partial(fine_kernel, masked),
        out_shape=(
            jax.ShapeDtypeStruct((TOK, width), BF),
            jax.ShapeDtypeStruct((TOK // 4, wide), BF),
        ),
        in_specs=[pl.BlockSpec(memory_space=pltpu.SMEM), vmem] + [hbm] * 5,
        out_specs=(vmem, vmem),
        scratch_shapes=[pltpu.VMEM(w.shape, BF) for w in weights]
        + [
            pltpu.VMEM((TOK, 3 * width), BF),
            pltpu.VMEM((TOK, width), BF),
            pltpu.VMEM((width // 128, TOK, 128), F32),
            pltpu.SemaphoreType.DMA((5,)),
        ],
        compiler_params=pltpu.CompilerParams(vmem_limit_bytes=40 << 20),
        cost_estimate=pl.CostEstimate(
            flops=flops, bytes_accessed=size + 3 * TOK * width * 2, transcendentals=TOK * 4 * width * 2
        ),
        name="fine_masked" if masked else "fine_plain",
    )(last, x, *weights)


def coarse_kernel(plan, last, table, x_ref, *rest):
    count = len(plan)
    pieces = rest[:count]
    out_ref = rest[count]
    vq, vp, qkv, mixed, sems = rest[count + 1:]
    a = vq.shape[1] // plan[0][3]
    b = vp.shape[1] // plan[0][3]
    first, second = [], []
    at = 0
    for ref, (groups, rows, _, _) in zip(pieces, plan):
        for g in range(groups):
            row = pl.multiple_of(table[2 * at], rows)
            lon = table[2 * at + 1]
            src = ref.at[pl.ds(g * rows, rows)]
            first.append(pltpu.make_async_copy(
                src.at[:, pl.ds(0, a)],
                vq.at[pl.ds(row, rows), pl.ds(pl.multiple_of(lon * a, 128), a)], sems.at[0]))
            second.append(pltpu.make_async_copy(
                src.at[:, pl.ds(a, b)],
                vp.at[pl.ds(row, rows), pl.ds(pl.multiple_of(lon * b, 128), b)], sems.at[1]))
            at += 1
    for copy in first:
        copy.start()
    for copy in second:
        copy.start()
    width = x_ref.shape[1]
    x = x_ref[...].astype(F32)
    normed = norm(x)
    for copy in first:
        copy.wait()
    step = width // 2
    for at in range(0, 3 * width, step):
        qkv[:, at:at + step] = dot(normed, vq[:, at:at + step]).astype(BF)
    attention(qkv, mixed, width, mask_bias(last))
    for copy in second:
        copy.wait()
    for at in range(0, width, step):
        cols = slice(at, at + step)
        out_ref[:, cols] = (x[:, cols] + dot(mixed[...], vp[:, cols])).astype(BF)


def coarse_window(x, last, table, pieces, plan, a, b):
    width = x.shape[-1]
    hbm = pl.BlockSpec(memory_space=pl.ANY)
    vmem = pl.BlockSpec(memory_space=pltpu.VMEM)
    smem = pl.BlockSpec(memory_space=pltpu.SMEM)
    return pl.pallas_call(
        functools.partial(coarse_kernel, plan),
        out_shape=jax.ShapeDtypeStruct((TOK, width), BF),
        in_specs=[smem, smem, vmem] + [hbm] * len(pieces),
        out_specs=vmem,
        scratch_shapes=[
            pltpu.VMEM((width, 3 * width), BF),
            pltpu.VMEM((width, width), BF),
            pltpu.VMEM((TOK, 3 * width), BF),
            pltpu.VMEM((TOK, width), BF),
            pltpu.SemaphoreType.DMA((2,)),
        ],
        compiler_params=pltpu.CompilerParams(vmem_limit_bytes=40 << 20),
        cost_estimate=pl.CostEstimate(
            flops=8 * TOK * width * width, bytes_accessed=8 * width * width, transcendentals=TOK * TOK * 16
        ),
        name="coarse",
    )(last, table, x, *pieces)


def line_ring(count):
    return [0] + list(range(1, count, 2)) + list(range(2, count, 2))[::-1]


def moves(order):
    place = {p: i for i, p in enumerate(order)}
    return lambda p, by: order[(place[p] + by) % len(order)]


def send(value, m, n, target):
    pairs = []
    for la in range(m):
        for lo in range(n):
            ta, to = target(la, lo)
            pairs.append((la * n + lo, ta * n + to))
    return lax.ppermute(value, ("lat", "lon"), pairs)


def gather_weights(shard, m, n):
    rows = shard.shape[0] // m
    places = n // 2
    along = moves(line_ring(places))
    across = moves(line_ring(m))
    part = lax.dynamic_slice_in_dim(shard, lax.axis_index("lat") * rows, rows, 0)
    got = []
    for _ in range(places - 1):
        part = send(part, m, n, lambda la, lo: (la, 2 * along(lo // 2, 1) + lo % 2))
        got.append(part)
    planes = [jnp.concatenate(got, axis=0)]
    for _ in range(m - 1):
        planes.append(send(planes[-1], m, n, lambda la, lo: (across(la, 1 - 2 * (lo % 2)), lo)))
    mine = [shard] + planes
    theirs = [send(piece, m, n, lambda la, lo: (la, lo ^ 1)) for piece in mine]
    tables = np.zeros((m, n, 2 * (1 + m * (places - 1)), 2), np.int32)
    for la in range(m):
        for lo in range(n):
            out = []
            for who in (lo, lo ^ 1):
                out.append((0, who))
                for k in range(m):
                    owner = across(la, -k * (1 - 2 * (who % 2)))
                    for s in range(1, places):
                        out.append((owner * rows, 2 * along(who // 2, -s) + who % 2))
            tables[la, lo] = out
    table = jnp.asarray(tables.reshape(m * n, -1))[lax.axis_index("lat") * n + lax.axis_index("lon")]
    plan = [(1, shard.shape[0], 0, n)] + [(places - 1, rows, 0, n)] * m
    return mine + theirs, tuple(plan + plan), table


def shifted(value, axis, steps):
    count = lax.axis_size(axis)
    return lax.ppermute(value, axis, [(s, (s + steps) % count) for s in range(count)])


def body(field, qkv_fine, proj_fine, up_fine, down_fine, merge_weight, qkv_coarse, proj_coarse):
    rows, cols, width = field.shape
    wide = merge_weight.shape[1]
    m = lax.axis_size("lat")
    n = lax.axis_size("lon")
    wr, wc = rows // WIN, cols // WIN
    last = (lax.axis_index("lat") == m - 1).astype(jnp.int32).reshape(1)
    fine_weights = (qkv_fine, proj_fine, up_fine, down_fine, merge_weight)

    east = shifted(field[:, :HALF], "lon", -1)
    widened = jnp.concatenate([field[:HALF, HALF:], east[:HALF]], axis=1)
    south = shifted(widened, "lat", -1)
    a, b = qkv_coarse.shape[1], proj_coarse.shape[1]
    if a % 128 == 0 and b % 128 == 0 and n % 2 == 0 and wide % (16 * m) == 0:
        pieces, plan, table = gather_weights(jnp.concatenate([qkv_coarse, proj_coarse], axis=1), m, n)
    else:
        whole = [lax.all_gather(w, "lon", axis=1, tiled=True) for w in (qkv_coarse, proj_coarse)]
        pieces, plan, table = [jnp.concatenate(whole, axis=1)], ((1, wide, 0, 1),), jnp.zeros((2,), jnp.int32)
        a, b = a * n, b * n

    def window(i, j):
        top, left = HALF + i * WIN, HALF + j * WIN
        if i < wr - 1:
            block = field[top:top + WIN, left:left + WIN]
            if j == wc - 1:
                block = jnp.concatenate([block, east[top:top + WIN]], axis=1)
        else:
            block = field[top:, left:left + WIN]
            if j == wc - 1:
                block = jnp.concatenate([block, east[top:]], axis=1)
            block = jnp.concatenate([block, south[:, j * WIN:(j + 1) * WIN]], axis=0)
        return block.reshape(TOK, width)

    fine, merged = {}, {}
    for i in range(wr):
        for j in range(wc):
            out, mer = fine_window(window(i, j), last, fine_weights, i == wr - 1)
            fine[i, j] = out.reshape(WIN, WIN, width)
            merged[i, j] = mer.reshape(HALF, HALF, wide)

    def lay(parts):
        return jnp.concatenate(
            [jnp.concatenate([parts[i, j] for j in range(wc)], axis=1) for i in range(wr)], axis=0
        )

    coarse = lay(merged)
    below = shifted(coarse[:QUART], "lat", -1)
    tall = jnp.concatenate([coarse[QUART:], below], axis=0)
    beside = shifted(tall[:, :QUART], "lon", -1)
    coarse = jnp.concatenate([tall[:, QUART:], beside], axis=1)

    def back(values):
        prev = shifted(values[-HALF:], "lat", 1)
        tall = jnp.concatenate([prev, values[:-HALF]], axis=0)
        side = shifted(tall[:, -HALF:], "lon", 1)
        return jnp.concatenate([side, tall[:, :-HALF]], axis=1)

    fine_out = back(lay(fine))
    cr, cc = rows // 2 // WIN, cols // 2 // WIN
    outs = {}
    for i in range(cr):
        for j in range(cc):
            block = coarse[i * WIN:(i + 1) * WIN, j * WIN:(j + 1) * WIN].reshape(TOK, wide)
            seam = last if i == cr - 1 else jnp.zeros_like(last)
            out = coarse_window(block, seam, table, pieces, plan, a, b)
            outs[i, j] = out.reshape(WIN, WIN, wide)
    coarse_out = jnp.concatenate(
        [jnp.concatenate([outs[i, j] for j in range(cc)], axis=1) for i in range(cr)], axis=0
    )
    return fine_out, back(coarse_out)


def solution(mesh):
    in_specs = (P("lat", "lon", None), P(), P(), P(), P(), P(), P(None, "lon"), P(None, "lon"))
    out_specs = (P("lat", "lon", None), P("lat", "lon", None))
    return jax.shard_map(body, mesh=mesh, in_specs=in_specs, out_specs=out_specs, check_vma=False)
```

```python
import functools

import jax
import jax.numpy as jnp
import numpy as np
from jax import lax
from jax.experimental import pallas as pl
from jax.experimental.pallas import tpu as pltpu
from jax.sharding import PartitionSpec as P

HEAD = 64
WIN = 16
HALF = WIN // 2
QUART = HALF // 2
TOK = WIN * WIN
SLAB = 2 * HEAD
NEG = -1e30
BF = jnp.bfloat16
F32 = jnp.float32


def dot(a, b):
    return jnp.dot(a, b, preferred_element_type=F32)


def norm(values):
    center = values - jnp.mean(values, axis=-1, keepdims=True)
    spread = jnp.mean(center * center, axis=-1, keepdims=True)
    return (center * lax.rsqrt(spread + 1e-05)).astype(BF)


def slab_attention(qkv, mixed, at, width, bias):
    q = qkv[:, pl.ds(at, SLAB)] * BF(HEAD ** (-0.5))
    k = qkv[:, pl.ds(at + width, SLAB)]
    v = qkv[:, pl.ds(at + 2 * width, SLAB)]
    low = lax.broadcasted_iota(jnp.int32, (TOK, SLAB), 1) < HEAD
    zero = jnp.zeros_like(q)
    one = jnp.ones_like(v)
    outs = []
    for qh, vh in (
        (jnp.where(low, q, zero), jnp.where(low, v, one)),
        (jnp.where(low, zero, q), jnp.where(low, one, v)),
    ):
        scores = lax.dot_general(qh, k, (((1,), (1,)), ((), ())), preferred_element_type=F32)
        if bias is not None:
            scores = scores + bias
        top = jnp.max(scores, axis=-1, keepdims=True)
        outs.append(dot(jnp.exp(scores - top).astype(BF), vh))
    sums = pltpu.roll(jnp.where(low, outs[1], outs[0]), HEAD, 1)
    mixed[:, pl.ds(at, SLAB)] = (jnp.where(low, outs[0], outs[1]) / sums).astype(BF)


def attention(qkv, mixed, width, bias):
    for at in range(0, width, SLAB):
        slab_attention(qkv, mixed, at, width, bias)


def mask_bias(last_ref):
    lead = lax.broadcasted_iota(jnp.int32, (TOK, TOK), 0) < TOK // 2
    other = lax.broadcasted_iota(jnp.int32, (TOK, TOK), 1) < TOK // 2
    return jnp.where(lead == other, 0.0, jnp.where(last_ref[0] > 0, NEG, 0.0))


def fine_kernel(masked, last, x_ref, vq, vp, vu, vd, vm, out_ref, merged_ref, qkv, mixed, wide):
    width = x_ref.shape[1]
    x = x_ref[...].astype(F32)
    normed = norm(x)
    for part in range(3):
        cols = slice(part * width, (part + 1) * width)
        qkv[:, cols] = dot(normed, vq[:, cols]).astype(BF)
    attention(qkv, mixed, width, mask_bias(last) if masked else None)
    attended = (x + dot(mixed[...], vp[...])).astype(BF).astype(F32)
    normed = norm(attended)
    total = attended
    step = width
    for at in range(0, vu.shape[1], step):
        hidden = jax.nn.gelu(dot(normed, vu[:, at:at + step])).astype(BF)
        total = total + dot(hidden, vd[at:at + step, :])
    fine = total.astype(BF)
    out_ref[...] = fine
    for c in range(width // 128):
        wide[c] = fine[:, c * 128:(c + 1) * 128].astype(F32)
    groups = []
    for b in range(2):
        picked = jnp.concatenate(
            [wide[c, pl.ds(b, TOK // 2, stride=2), :] for c in range(width // 128)], axis=1
        ).reshape(HALF, 2, HALF, width)
        groups.append((picked[:, 0].reshape(TOK // 4, width), picked[:, 1].reshape(TOK // 4, width)))
    joined = [groups[0][0], groups[0][1], groups[1][0], groups[1][1]]
    count = 4 * width
    mean = sum(jnp.sum(g, axis=-1, keepdims=True) for g in joined) / count
    joined = [g - mean for g in joined]
    spread = sum(jnp.sum(g * g, axis=-1, keepdims=True) for g in joined) / count
    scale = lax.rsqrt(spread + 1e-05)
    merged = 0.0
    for i, g in enumerate(joined):
        merged = merged + dot((g * scale).astype(BF), vm[i * width:(i + 1) * width, :])
    merged_ref[...] = merged.astype(BF)


def fine_window(x, last, weights, masked):
    width = x.shape[-1]
    wide = weights[-1].shape[1]
    flops = 2 * TOK * width * (3 * width + width + 4 * width * 2) + TOK * 2 * width * wide
    size = sum(w.size * 2 for w in weights)
    vmem = pl.BlockSpec(memory_space=pltpu.VMEM)
    return pl.pallas_call(
        functools.partial(fine_kernel, masked),
        out_shape=(
            jax.ShapeDtypeStruct((TOK, width), BF),
            jax.ShapeDtypeStruct((TOK // 4, wide), BF),
        ),
        in_specs=[pl.BlockSpec(memory_space=pltpu.SMEM), vmem] + [vmem] * 5,
        out_specs=(vmem, vmem),
        scratch_shapes=[
            pltpu.VMEM((TOK, 3 * width), BF),
            pltpu.VMEM((TOK, width), BF),
            pltpu.VMEM((width // 128, TOK, 128), F32),
        ],
        compiler_params=pltpu.CompilerParams(vmem_limit_bytes=24 << 20),
        cost_estimate=pl.CostEstimate(
            flops=flops, bytes_accessed=size + 3 * TOK * width * 2, transcendentals=TOK * 4 * width * 2
        ),
        name="fine_masked" if masked else "fine_plain",
    )(last, x, *weights)


def coarse_kernel(plan, last, table, x_ref, *rest):
    count = len(plan)
    pieces = rest[:count]
    out_ref, xn, qkv, mixed = rest[count:]
    width = x_ref.shape[1]
    x = x_ref[...].astype(F32)
    xn[...] = norm(x)

    def project(source, target, which):
        for group, refs, start in plan_groups(plan, pieces, which):
            total = 0.0
            for slot, ref, cols in refs:
                rows = ref.shape[0]
                if rows == width:
                    lhs = source[...]
                else:
                    lhs = source[:, pl.ds(pl.multiple_of(table[2 * slot], rows), rows)]
                total = total + dot(lhs, ref[:, cols])
            size = total.shape[1]
            at = pl.multiple_of(table[2 * group + 1] * size, 128)
            target(pl.ds(at, size), total)

    def keep(cols, total):
        qkv[:, cols] = total.astype(BF)

    def finish(cols, total):
        out_ref[:, cols] = (x_ref[:, cols].astype(F32) + total).astype(BF)

    project(xn, keep, 0)
    attention(qkv, mixed, width, mask_bias(last))
    project(mixed, finish, 1)


def plan_groups(plan, pieces, which):
    shards = {}
    for slot, (shard, cols) in enumerate(plan):
        if cols[which] is not None:
            shards.setdefault(shard, []).append((slot, pieces[slot], slice(*cols[which])))
    return [(refs[0][0], refs, 0) for refs in shards.values()]


def coarse_window(x, last, table, pieces, plan):
    width = x.shape[-1]
    vmem = pl.BlockSpec(memory_space=pltpu.VMEM)
    smem = pl.BlockSpec(memory_space=pltpu.SMEM)
    return pl.pallas_call(
        functools.partial(coarse_kernel, plan),
        out_shape=jax.ShapeDtypeStruct((TOK, width), BF),
        in_specs=[smem, smem, vmem] + [vmem] * len(pieces),
        out_specs=vmem,
        scratch_shapes=[
            pltpu.VMEM((TOK, width), BF),
            pltpu.VMEM((TOK, 3 * width), BF),
            pltpu.VMEM((TOK, width), BF),
        ],
        compiler_params=pltpu.CompilerParams(vmem_limit_bytes=24 << 20),
        cost_estimate=pl.CostEstimate(
            flops=8 * TOK * width * width, bytes_accessed=8 * width * width, transcendentals=TOK * TOK * 16
        ),
        name="coarse",
    )(last, table, x, *pieces)


def line_ring(count):
    return [0] + list(range(1, count, 2)) + list(range(2, count, 2))[::-1]


def moves(order):
    place = {p: i for i, p in enumerate(order)}
    return lambda p, by: order[(place[p] + by) % len(order)]


def send(value, m, n, target):
    pairs = []
    for la in range(m):
        for lo in range(n):
            ta, to = target(la, lo)
            pairs.append((la * n + lo, ta * n + to))
    return lax.ppermute(value, ("lat", "lon"), pairs)


def gather_weights(qkv_shard, proj_shard, m, n):
    deep = qkv_shard.shape[0]
    a, b = qkv_shard.shape[1], proj_shard.shape[1]
    rows = deep // 2
    places = n // 2
    along = moves(line_ring(places))
    ring = line_ring(m)
    across = moves(ring)
    side = jnp.asarray(np.array([ring.index(la) % 2 for la in range(m)], np.int32))[lax.axis_index("lat")]
    part = jnp.concatenate(
        [lax.dynamic_slice_in_dim(w, side * rows, rows, 0) for w in (qkv_shard, proj_shard)], axis=1
    )
    pieces = [qkv_shard, proj_shard]
    plan = [("own", ((0, a), None)), ("own", (None, (0, b)))]

    def swap(value):
        return send(value, m, n, lambda la, lo: (la, lo ^ 1))

    pieces += [swap(qkv_shard), swap(proj_shard)]
    plan += [("peer", ((0, a), None)), ("peer", (None, (0, b)))]
    whole = ((0, a), (a, a + b))
    for s in range(1, places):
        part = send(part, m, n, lambda la, lo: (la, 2 * along(lo // 2, 1) + lo % 2))
        other = send(part, m, n, lambda la, lo: (across(la, 1 - 2 * (lo % 2)), lo))
        pieces += [part, other, swap(part), swap(other)]
        plan += [(s, whole), (s, whole), (-s, whole), (-s, whole)]
    tables = np.zeros((m, n, len(pieces), 2), np.int32)
    for la in range(m):
        for lo in range(n):
            mine = ring.index(la) % 2
            out = [(0, lo), (0, lo), (0, lo ^ 1), (0, lo ^ 1)]
            for s in range(1, places):
                for who in (lo, lo ^ 1):
                    lon = 2 * along(who // 2, -s) + who % 2
                    out += [(mine * rows, lon), ((1 - mine) * rows, lon)]
            tables[la, lo] = out
    table = jnp.asarray(tables.reshape(m * n, -1))[lax.axis_index("lat") * n + lax.axis_index("lon")]
    return pieces, tuple(plan), table


def shifted(value, axis, steps):
    count = lax.axis_size(axis)
    return lax.ppermute(value, axis, [(s, (s + steps) % count) for s in range(count)])


def whole_body(field, qkv_fine, proj_fine, up_fine, down_fine, merge_weight, qkv_coarse, proj_coarse):
    rows, cols, width = field.shape
    wide = merge_weight.shape[1]
    m = lax.axis_size("lat")
    n = lax.axis_size("lon")
    wr, wc = rows // WIN, cols // WIN
    last = (lax.axis_index("lat") == m - 1).astype(jnp.int32).reshape(1)
    fine_weights = (qkv_fine, proj_fine, up_fine, down_fine, merge_weight)

    east = shifted(field[:, :HALF], "lon", -1)
    widened = jnp.concatenate([field[:HALF, HALF:], east[:HALF]], axis=1)
    south = shifted(widened, "lat", -1)
    a, b = qkv_coarse.shape[1], proj_coarse.shape[1]
    if a % 128 == 0 and b % 128 == 0 and n % 2 == 0 and m % 2 == 0:
        pieces, plan, table = gather_weights(qkv_coarse, proj_coarse, m, n)
    else:
        pieces = [lax.all_gather(w, "lon", axis=1, tiled=True) for w in (qkv_coarse, proj_coarse)]
        plan = ((0, ((0, a * n), None)), (0, (None, (0, b * n))))
        table = jnp.zeros((4,), jnp.int32)

    def window(i, j):
        top, left = HALF + i * WIN, HALF + j * WIN
        if i < wr - 1:
            block = field[top:top + WIN, left:left + WIN]
            if j == wc - 1:
                block = jnp.concatenate([block, east[top:top + WIN]], axis=1)
        else:
            block = field[top:, left:left + WIN]
            if j == wc - 1:
                block = jnp.concatenate([block, east[top:]], axis=1)
            block = jnp.concatenate([block, south[:, j * WIN:(j + 1) * WIN]], axis=0)
        return block.reshape(TOK, width)

    fine, merged = {}, {}
    for i in range(wr):
        for j in range(wc):
            out, mer = fine_window(window(i, j), last, fine_weights, i == wr - 1)
            fine[i, j] = out.reshape(WIN, WIN, width)
            merged[i, j] = mer.reshape(HALF, HALF, wide)

    def lay(parts):
        return jnp.concatenate(
            [jnp.concatenate([parts[i, j] for j in range(wc)], axis=1) for i in range(wr)], axis=0
        )

    coarse = lay(merged)
    below = shifted(coarse[:QUART], "lat", -1)
    tall = jnp.concatenate([coarse[QUART:], below], axis=0)
    beside = shifted(tall[:, :QUART], "lon", -1)
    coarse = jnp.concatenate([tall[:, QUART:], beside], axis=1)

    def back(values):
        down = lambda la: (la + 1) % m
        right = lambda lo: (lo + 1) % n
        side = send(values[:-HALF, -HALF:], m, n, lambda la, lo: (la, right(lo)))
        prev = send(values[-HALF:, :-HALF], m, n, lambda la, lo: (down(la), lo))
        corner = send(values[-HALF:, -HALF:], m, n, lambda la, lo: (down(la), right(lo)))
        top = jnp.concatenate([corner, prev], axis=1)
        return jnp.concatenate([top, jnp.concatenate([side, values[:-HALF, :-HALF]], axis=1)], axis=0)

    fine_out = back(lay(fine))
    cr, cc = rows // 2 // WIN, cols // 2 // WIN
    outs = {}
    for i in range(cr):
        for j in range(cc):
            block = coarse[i * WIN:(i + 1) * WIN, j * WIN:(j + 1) * WIN].reshape(TOK, wide)
            seam = last if i == cr - 1 else jnp.zeros_like(last)
            out = coarse_window(block, seam, table, pieces, plan)
            outs[i, j] = out.reshape(WIN, WIN, wide)
    coarse_out = jnp.concatenate(
        [jnp.concatenate([outs[i, j] for j in range(cc)], axis=1) for i in range(cr)], axis=0
    )
    return fine_out, back(coarse_out)


def solution(mesh):
    in_specs = (P("lat", "lon", None), P(), P(), P(), P(), P(), P(None, "lon"), P(None, "lon"))
    out_specs = (P("lat", "lon", None), P("lat", "lon", None))
    return jax.shard_map(whole_body, mesh=mesh, in_specs=in_specs, out_specs=out_specs, check_vma=False)
```

```python
import functools

import jax
import jax.numpy as jnp
import numpy as np
from jax import lax
from jax.experimental import pallas as pl
from jax.experimental.pallas import tpu as pltpu
from jax.sharding import PartitionSpec as P

HEAD = 64
WIN = 16
HALF = WIN // 2
QUART = HALF // 2
TOK = WIN * WIN
SLAB = 2 * HEAD
NEG = -1e30
BF = jnp.bfloat16
F32 = jnp.float32


def dot(a, b):
    return jnp.dot(a, b, preferred_element_type=F32)


def norm(values):
    center = values - jnp.mean(values, axis=-1, keepdims=True)
    spread = jnp.mean(center * center, axis=-1, keepdims=True)
    return (center * lax.rsqrt(spread + 1e-05)).astype(BF)


def slab_attention(qkv, mixed, at, width, bias):
    q = qkv[:, pl.ds(at, SLAB)] * BF(HEAD ** (-0.5))
    k = qkv[:, pl.ds(at + width, SLAB)]
    v = qkv[:, pl.ds(at + 2 * width, SLAB)]
    low = lax.broadcasted_iota(jnp.int32, (TOK, SLAB), 1) < HEAD
    zero = jnp.zeros_like(q)
    one = jnp.ones_like(v)
    outs = []
    for qh, vh in (
        (jnp.where(low, q, zero), jnp.where(low, v, one)),
        (jnp.where(low, zero, q), jnp.where(low, one, v)),
    ):
        scores = lax.dot_general(qh, k, (((1,), (1,)), ((), ())), preferred_element_type=F32)
        if bias is not None:
            scores = scores + bias
        top = jnp.max(scores, axis=-1, keepdims=True)
        outs.append(dot(jnp.exp(scores - top).astype(BF), vh))
    sums = pltpu.roll(jnp.where(low, outs[1], outs[0]), HEAD, 1)
    mixed[:, pl.ds(at, SLAB)] = (jnp.where(low, outs[0], outs[1]) / sums).astype(BF)


def attention(qkv, mixed, width, bias):
    for at in range(0, width, SLAB):
        slab_attention(qkv, mixed, at, width, bias)


def mask_bias(last_ref):
    lead = lax.broadcasted_iota(jnp.int32, (TOK, TOK), 0) < TOK // 2
    other = lax.broadcasted_iota(jnp.int32, (TOK, TOK), 1) < TOK // 2
    return jnp.where(lead == other, 0.0, jnp.where(last_ref[0] > 0, NEG, 0.0))


def window_blocks(i, j, rows, cols):
    top, left = HALF + i * WIN, HALF + j * WIN
    tall = [(0, top, 0, min(WIN, rows - top))]
    wide = [(0, left, 0, min(WIN, cols - left))]
    if top + WIN > rows:
        tall.append((1, 0, HALF, HALF))
    if left + WIN > cols:
        wide.append((1, 0, HALF, HALF))
    out = []
    for below, r, to_r, count_r in tall:
        for beside, c, to_c, count_c in wide:
            source = ("field", "east", "south", "corner")[2 * below + beside]
            at_c = c - HALF if source == "south" else c
            out.append((source, r, at_c, to_r, to_c, count_r, count_c))
    return out


def fine_kernel(masked, first, names, blocks, last, *refs):
    count = len(names)
    sources = dict(zip(names, refs[:count]))
    weights, refs = refs[count:count + 5], refs[count + 5:]
    out_ref, merged_ref = refs[:2]
    qkv, mixed, wide, window, sems = refs[-5:]
    moves_in = []
    for at, (name, r, c, to_r, to_c, nr, nc) in enumerate(blocks):
        moves_in.append(pltpu.make_async_copy(
            sources[name].at[pl.ds(r, nr), pl.ds(c, nc)],
            window.at[pl.ds(to_r, nr), pl.ds(to_c, nc)], sems.at[at]))
    for copy in moves_in:
        copy.start()
    loads = []
    if first:
        held = refs[2:7]
        for at, (src, dst) in enumerate(zip(weights, held)):
            loads.append(pltpu.make_async_copy(src, dst, sems.at[4 + at]))
            loads[-1].start()
        weights = held
    vq, vp, vu, vd, vm = weights

    def ready(at):
        if first:
            loads[at].wait()

    for copy in moves_in:
        copy.wait()
    width = window.shape[2]
    x = window[...].reshape(TOK, width).astype(F32)
    normed = norm(x)
    ready(0)
    for part in range(3):
        cols = slice(part * width, (part + 1) * width)
        qkv[:, cols] = dot(normed, vq[:, cols]).astype(BF)
    attention(qkv, mixed, width, mask_bias(last) if masked else None)
    ready(1)
    attended = (x + dot(mixed[...], vp[...])).astype(BF).astype(F32)
    normed = norm(attended)
    ready(2)
    ready(3)
    total = attended
    step = width
    for at in range(0, vu.shape[1], step):
        hidden = jax.nn.gelu(dot(normed, vu[:, at:at + step])).astype(BF)
        total = total + dot(hidden, vd[at:at + step, :])
    fine = total.astype(BF)
    out_ref[...] = fine
    for c in range(width // 128):
        wide[c] = fine[:, c * 128:(c + 1) * 128].astype(F32)
    groups = []
    for b in range(2):
        picked = jnp.concatenate(
            [wide[c, pl.ds(b, TOK // 2, stride=2), :] for c in range(width // 128)], axis=1
        ).reshape(HALF, 2, HALF, width)
        groups.append((picked[:, 0].reshape(TOK // 4, width), picked[:, 1].reshape(TOK // 4, width)))
    joined = [groups[0][0], groups[0][1], groups[1][0], groups[1][1]]
    count = 4 * width
    mean = sum(jnp.sum(g, axis=-1, keepdims=True) for g in joined) / count
    joined = [g - mean for g in joined]
    spread = sum(jnp.sum(g * g, axis=-1, keepdims=True) for g in joined) / count
    scale = lax.rsqrt(spread + 1e-05)
    ready(4)
    merged = 0.0
    for i, g in enumerate(joined):
        merged = merged + dot((g * scale).astype(BF), vm[i * width:(i + 1) * width, :])
    merged_ref[...] = merged.astype(BF)


def fine_window(i, j, arrays, last, weights, masked, first):
    rows, cols, width = arrays["field"].shape
    wide = weights[-1].shape[1]
    blocks = window_blocks(i, j, rows, cols)
    names = tuple(dict.fromkeys(block[0] for block in blocks))
    flops = 2 * TOK * width * (3 * width + width + 4 * width * 2) + TOK * 2 * width * wide
    size = sum(w.size * 2 for w in weights)
    hbm = pl.BlockSpec(memory_space=pl.ANY)
    vmem = pl.BlockSpec(memory_space=pltpu.VMEM)
    held = [jax.ShapeDtypeStruct(w.shape, BF) for w in weights] if first else []
    return pl.pallas_call(
        functools.partial(fine_kernel, masked, first, names, blocks),
        out_shape=[
            jax.ShapeDtypeStruct((TOK, width), BF),
            jax.ShapeDtypeStruct((TOK // 4, wide), BF),
        ]
        + held,
        in_specs=[pl.BlockSpec(memory_space=pltpu.SMEM)] + [hbm] * len(names) + [hbm if first else vmem] * 5,
        out_specs=[vmem] * (2 + len(held)),
        scratch_shapes=[
            pltpu.VMEM((TOK, 3 * width), BF),
            pltpu.VMEM((TOK, width), BF),
            pltpu.VMEM((width // 128, TOK, 128), F32),
            pltpu.VMEM((WIN, WIN, width), BF),
            pltpu.SemaphoreType.DMA((9,)),
        ],
        compiler_params=pltpu.CompilerParams(vmem_limit_bytes=24 << 20),
        cost_estimate=pl.CostEstimate(
            flops=flops, bytes_accessed=size + 3 * TOK * width * 2, transcendentals=TOK * 4 * width * 2
        ),
        name="fine_first" if first else "fine_masked" if masked else "fine_plain",
    )(last, *[arrays[name] for name in names], *weights)


def cut_kernel(regions, offsets, *refs):
    count = (len(refs) - 1) // 2
    sems = refs[-1]
    copies = []
    for at, (src, dst, region) in enumerate(zip(refs[:count], refs[count:-1], regions)):
        where = []
        for start, size in region:
            if isinstance(start, str):
                start = pl.multiple_of(offsets[int(start)], size)
            where.append(pl.ds(start, size))
        copies.append(pltpu.make_async_copy(src.at[tuple(where)], dst, sems.at[at]))
    for copy in copies:
        copy.start()
    for copy in copies:
        copy.wait()


def cut(offsets, cuts):
    hbm = pl.BlockSpec(memory_space=pl.ANY)
    vmem = pl.BlockSpec(memory_space=pltpu.VMEM)
    shapes = [tuple(size for _, size in region) for _, region in cuts]
    return pl.pallas_call(
        functools.partial(cut_kernel, tuple(region for _, region in cuts)),
        out_shape=[jax.ShapeDtypeStruct(shape, BF) for shape in shapes],
        in_specs=[pl.BlockSpec(memory_space=pltpu.SMEM)] + [hbm] * len(cuts),
        out_specs=[vmem] * len(cuts),
        scratch_shapes=[pltpu.SemaphoreType.DMA((len(cuts),))],
        compiler_params=pltpu.CompilerParams(vmem_limit_bytes=8 << 20),
        cost_estimate=pl.CostEstimate(
            flops=0, bytes_accessed=sum(2 * int(np.prod(shape)) for shape in shapes), transcendentals=0
        ),
        name="cut",
    )(offsets, *[array for array, _ in cuts])


def coarse_kernel(plan, last, table, x_ref, *rest):
    count = max(entry[0] for entry in plan) + 1
    pieces = rest[:count]
    out_ref, xn, qkv, mixed, proj, sem = rest[count:]
    width = x_ref.shape[1]

    def place(slot, rows, columns):
        row = pl.multiple_of(table[2 * slot], rows)
        column = pl.multiple_of(table[2 * slot + 1] * columns, 128)
        return pl.ds(row, rows), pl.ds(column, columns)

    copies, shards = [], {}
    for slot, (piece, r, rows, c, columns, shard, which) in enumerate(plan):
        part = pieces[piece].at[pl.ds(r, rows), pl.ds(c, columns)]
        if which == 1:
            copies.append(pltpu.make_async_copy(part, proj.at[place(slot, rows, columns)], sem.at[len(copies)]))
        else:
            shards.setdefault(shard, []).append((slot, part, rows, columns))
    for copy in copies:
        copy.start()
    xn[...] = norm(x_ref[...].astype(F32))
    for parts in shards.values():
        total = 0.0
        for slot, part, rows, columns in parts:
            row, column = place(slot, rows, columns)
            lhs = xn[...] if rows == width else xn[:, row]
            total = total + dot(lhs, part[...])
        qkv[:, column] = total.astype(BF)
    attention(qkv, mixed, width, mask_bias(last))
    for copy in copies:
        copy.wait()
    step = width // 2
    for at in range(0, width, step):
        cols = slice(at, at + step)
        out_ref[:, cols] = (x_ref[:, cols].astype(F32) + dot(mixed[...], proj[:, cols])).astype(BF)


def coarse_window(x, last, table, pieces, plan):
    width = x.shape[-1]
    vmem = pl.BlockSpec(memory_space=pltpu.VMEM)
    smem = pl.BlockSpec(memory_space=pltpu.SMEM)
    return pl.pallas_call(
        functools.partial(coarse_kernel, plan),
        out_shape=jax.ShapeDtypeStruct((TOK, width), BF),
        in_specs=[smem, smem, vmem] + [vmem] * len(pieces),
        out_specs=vmem,
        scratch_shapes=[
            pltpu.VMEM((TOK, width), BF),
            pltpu.VMEM((TOK, 3 * width), BF),
            pltpu.VMEM((TOK, width), BF),
            pltpu.VMEM((width, width), BF),
            pltpu.SemaphoreType.DMA((sum(entry[6] for entry in plan),)),
        ],
        compiler_params=pltpu.CompilerParams(vmem_limit_bytes=24 << 20),
        cost_estimate=pl.CostEstimate(
            flops=8 * TOK * width * width, bytes_accessed=8 * width * width, transcendentals=TOK * TOK * 16
        ),
        name="coarse",
    )(last, table, x, *pieces)


def line_ring(count):
    return [0] + list(range(1, count, 2)) + list(range(2, count, 2))[::-1]


def moves(order):
    place = {p: i for i, p in enumerate(order)}
    return lambda p, by: order[(place[p] + by) % len(order)]


def send(value, m, n, target):
    pairs = []
    for la in range(m):
        for lo in range(n):
            ta, to = target(la, lo)
            pairs.append((la * n + lo, ta * n + to))
    return lax.ppermute(value, ("lat", "lon"), pairs)


def half_of(ring, la):
    return ring.index(la) % 2


def gather_weights(qkv_shard, proj_shard, qkv_part, proj_part, m, n):
    deep = qkv_shard.shape[0]
    a, b = qkv_shard.shape[1], proj_shard.shape[1]
    half, share = qkv_part.shape[0], proj_part.shape[0]
    places = n // 2
    along = moves(line_ring(places))
    ring = line_ring(m)
    across = moves(ring)
    turn = lambda lo: 1 - 2 * (lo % 2)
    origin = lambda lo, s: 2 * along(lo // 2, s) + lo % 2

    def swap(value):
        return send(value, m, n, lambda la, lo: (la, lo ^ 1))

    pieces, plan, spots = [], [], []

    def add(value, which, spot, columns, cuts):
        for twin in range(2):
            for r, rows, key in cuts:
                plan.append((len(pieces), r, rows, 0, columns, (twin, key), which))
                spots.append((twin, spot, key))
            pieces.append(swap(value) if twin else value)

    add(qkv_shard, 0, lambda la, lo, key: (0, lo), a, [(0, deep, 0)])
    add(proj_shard, 1, lambda la, lo, key: (0, lo), b, [(0, deep, 0)])
    part = qkv_part
    shares = []
    for s in range(1, places):
        part = send(part, m, n, lambda la, lo: (la, origin(lo, 1)))
        shares.append(send(proj_part, m, n, lambda la, lo: (la, origin(lo, s))))
        other = send(part, m, n, lambda la, lo: (across(la, turn(lo)), lo))
        for value, flip in ((part, 0), (other, 1)):
            spot = lambda la, lo, key, flip=flip: ((half_of(ring, la) ^ flip) * half, origin(lo, -key))
            add(value, 0, spot, a, [(0, half, s)])
    plane = jnp.concatenate(shares, axis=0)
    for k in range(m):
        if k > 0:
            plane = send(plane, m, n, lambda la, lo: (across(la, turn(lo)), lo))
        spot = lambda la, lo, key, k=k: (across(la, -k * turn(lo)) * share, origin(lo, -key))
        add(plane, 1, spot, b, [((s - 1) * share, share, s) for s in range(1, places)])
    tables = np.zeros((m, n, len(spots), 2), np.int32)
    for la in range(m):
        for lo in range(n):
            tables[la, lo] = [spot(la, lo ^ twin, key) for twin, spot, key in spots]
    table = jnp.asarray(tables.reshape(m * n, -1))[lax.axis_index("lat") * n + lax.axis_index("lon")]
    return pieces, tuple(plan), table


def shifted(value, axis, steps):
    count = lax.axis_size(axis)
    return lax.ppermute(value, axis, [(s, (s + steps) % count) for s in range(count)])


def whole_body(field, qkv_fine, proj_fine, up_fine, down_fine, merge_weight, qkv_coarse, proj_coarse):
    rows, cols, width = field.shape
    wide = merge_weight.shape[1]
    m = lax.axis_size("lat")
    n = lax.axis_size("lon")
    wr, wc = rows // WIN, cols // WIN
    last = (lax.axis_index("lat") == m - 1).astype(jnp.int32).reshape(1)
    fine_weights = (qkv_fine, proj_fine, up_fine, down_fine, merge_weight)

    deep, a = qkv_coarse.shape
    b = proj_coarse.shape[1]
    direct = a % 128 == 0 and b % 128 == 0 and n % 2 == 0 and m % 2 == 0 and deep % (16 * m) == 0
    cuts = [
        (field, ((0, rows), (0, HALF), (0, width))),
        (field, ((0, HALF), (HALF, cols - HALF), (0, width))),
        (field, ((0, HALF), (0, HALF), (0, width))),
    ]
    lat = lax.axis_index("lat")
    ring = line_ring(m)
    offsets = jnp.asarray(
        np.array([(half_of(ring, la) * (deep // 2), la * (deep // m)) for la in range(m)], np.int32)
    )[lat]
    if direct:
        cuts += [(qkv_coarse, (("0", deep // 2), (0, a))), (proj_coarse, (("1", deep // m), (0, b)))]
    parts = cut(offsets, cuts)
    up = lambda la: (la - 1) % m
    left = lambda lo: (lo - 1) % n
    arrays = {"field": field}
    arrays["east"] = send(parts[0], m, n, lambda la, lo: (la, left(lo)))
    arrays["south"] = send(parts[1], m, n, lambda la, lo: (up(la), lo))
    arrays["corner"] = send(parts[2], m, n, lambda la, lo: (up(la), left(lo)))
    if direct:
        pieces, plan, table = gather_weights(qkv_coarse, proj_coarse, parts[3], parts[4], m, n)
    else:
        pieces = [lax.all_gather(w, "lon", axis=1, tiled=True) for w in (qkv_coarse, proj_coarse)]
        plan = ((0, 0, deep, 0, a * n, 0, 0), (1, 0, deep, 0, b * n, 0, 1))
        table = jnp.zeros((4,), jnp.int32)

    fine, merged = {}, {}
    held = fine_weights
    for i in range(wr):
        for j in range(wc):
            first = i == 0 and j == 0
            out, mer, *kept = fine_window(i, j, arrays, last, held, i == wr - 1, first)
            held = kept if first else held
            fine[i, j] = out.reshape(WIN, WIN, width)
            merged[i, j] = mer.reshape(HALF, HALF, wide)

    def lay(parts):
        return jnp.concatenate(
            [jnp.concatenate([parts[i, j] for j in range(wc)], axis=1) for i in range(wr)], axis=0
        )

    top = jnp.concatenate([merged[0, j][:QUART] for j in range(wc)], axis=1)
    below = shifted(top, "lat", -1)
    side = jnp.concatenate([merged[i, 0][:, :QUART] for i in range(wr)], axis=0)
    side = jnp.concatenate([side[QUART:], below[:, :QUART]], axis=0)
    beside = shifted(side, "lon", -1)
    tall = jnp.concatenate([lay(merged)[QUART:], below], axis=0)
    coarse = jnp.concatenate([tall[:, QUART:], beside], axis=1)

    def back(values):
        down = lambda la: (la + 1) % m
        right = lambda lo: (lo + 1) % n
        side = send(values[:-HALF, -HALF:], m, n, lambda la, lo: (la, right(lo)))
        prev = send(values[-HALF:, :-HALF], m, n, lambda la, lo: (down(la), lo))
        corner = send(values[-HALF:, -HALF:], m, n, lambda la, lo: (down(la), right(lo)))
        top = jnp.concatenate([corner, prev], axis=1)
        return jnp.concatenate([top, jnp.concatenate([side, values[:-HALF, :-HALF]], axis=1)], axis=0)

    fine_out = back(lay(fine))
    cr, cc = rows // 2 // WIN, cols // 2 // WIN
    outs = {}
    for i in range(cr):
        for j in range(cc):
            block = coarse[i * WIN:(i + 1) * WIN, j * WIN:(j + 1) * WIN].reshape(TOK, wide)
            seam = last if i == cr - 1 else jnp.zeros_like(last)
            out = coarse_window(block, seam, table, pieces, plan)
            outs[i, j] = out.reshape(WIN, WIN, wide)
    coarse_out = jnp.concatenate(
        [jnp.concatenate([outs[i, j] for j in range(cc)], axis=1) for i in range(cr)], axis=0
    )
    return fine_out, back(coarse_out)


def solution(mesh):
    in_specs = (P("lat", "lon", None), P(), P(), P(), P(), P(), P(None, "lon"), P(None, "lon"))
    out_specs = (P("lat", "lon", None), P("lat", "lon", None))
    return jax.shard_map(whole_body, mesh=mesh, in_specs=in_specs, out_specs=out_specs, check_vma=False)
```

```python
import functools

import jax
import jax.numpy as jnp
import numpy as np
from jax import lax
from jax.experimental import pallas as pl
from jax.experimental.pallas import tpu as pltpu
from jax.sharding import PartitionSpec as P

HEAD = 64
WIN = 16
HALF = WIN // 2
QUART = HALF // 2
TOK = WIN * WIN
SLAB = 2 * HEAD
NEG = -1e30
BF = jnp.bfloat16
F32 = jnp.float32


def dot(a, b):
    return jnp.dot(a, b, preferred_element_type=F32)


def norm(values):
    center = values - jnp.mean(values, axis=-1, keepdims=True)
    spread = jnp.mean(center * center, axis=-1, keepdims=True)
    return (center * lax.rsqrt(spread + 1e-05)).astype(BF)


def slab_attention(qkv, mixed, at, width, bias):
    q = qkv[:, pl.ds(at, SLAB)] * BF(HEAD ** (-0.5))
    k = qkv[:, pl.ds(at + width, SLAB)]
    v = qkv[:, pl.ds(at + 2 * width, SLAB)]
    low = lax.broadcasted_iota(jnp.int32, (TOK, SLAB), 1) < HEAD
    zero = jnp.zeros_like(q)
    one = jnp.ones_like(v)
    outs = []
    for qh, vh in (
        (jnp.where(low, q, zero), jnp.where(low, v, one)),
        (jnp.where(low, zero, q), jnp.where(low, one, v)),
    ):
        scores = lax.dot_general(qh, k, (((1,), (1,)), ((), ())), preferred_element_type=F32)
        if bias is not None:
            scores = scores + bias
        top = jnp.max(scores, axis=-1, keepdims=True)
        outs.append(dot(jnp.exp(scores - top).astype(BF), vh))
    sums = pltpu.roll(jnp.where(low, outs[1], outs[0]), HEAD, 1)
    mixed[:, pl.ds(at, SLAB)] = (jnp.where(low, outs[0], outs[1]) / sums).astype(BF)


def attention(qkv, mixed, width, bias):
    for at in range(0, width, SLAB):
        slab_attention(qkv, mixed, at, width, bias)


def mask_bias(last_ref):
    lead = lax.broadcasted_iota(jnp.int32, (TOK, TOK), 0) < TOK // 2
    other = lax.broadcasted_iota(jnp.int32, (TOK, TOK), 1) < TOK // 2
    return jnp.where(lead == other, 0.0, jnp.where(last_ref[0] > 0, NEG, 0.0))


def window_blocks(i, j, rows, cols):
    top, left = HALF + i * WIN, HALF + j * WIN
    tall = [(0, top, 0, min(WIN, rows - top))]
    wide = [(0, left, 0, min(WIN, cols - left))]
    if top + WIN > rows:
        tall.append((1, 0, HALF, HALF))
    if left + WIN > cols:
        wide.append((1, 0, HALF, HALF))
    out = []
    for below, r, to_r, count_r in tall:
        for beside, c, to_c, count_c in wide:
            source = ("field", "east", "south", "corner")[2 * below + beside]
            at_c = c - HALF if source == "south" else c
            out.append((source, r, at_c, to_r, to_c, count_r, count_c))
    return out


def fine_kernel(masked, first, names, blocks, last, *refs):
    count = len(names)
    sources = dict(zip(names, refs[:count]))
    weights, refs = refs[count:count + 5], refs[count + 5:]
    out_ref, merged_ref = refs[:2]
    qkv, mixed, wide, window, sems = refs[-5:]
    loads = []
    if first:
        held = refs[2:7]
        for at, (src, dst) in enumerate(zip(weights, held)):
            loads.append(pltpu.make_async_copy(src, dst, sems.at[at]))
            loads[-1].start()
        weights = held
    vq, vp, vu, vd, vm = weights

    def ready(at):
        if first:
            loads[at].wait()

    for name, r, c, to_r, to_c, nr, nc in blocks:
        window[to_r:to_r + nr, to_c:to_c + nc] = sources[name][r:r + nr, c:c + nc]
    width = window.shape[2]
    x = window[...].reshape(TOK, width).astype(F32)
    normed = norm(x)
    ready(0)
    for part in range(3):
        cols = slice(part * width, (part + 1) * width)
        qkv[:, cols] = dot(normed, vq[:, cols]).astype(BF)
    attention(qkv, mixed, width, mask_bias(last) if masked else None)
    ready(1)
    attended = (x + dot(mixed[...], vp[...])).astype(BF).astype(F32)
    normed = norm(attended)
    ready(2)
    ready(3)
    total = attended
    step = width
    for at in range(0, vu.shape[1], step):
        hidden = jax.nn.gelu(dot(normed, vu[:, at:at + step])).astype(BF)
        total = total + dot(hidden, vd[at:at + step, :])
    fine = total.astype(BF)
    out_ref[...] = fine
    for c in range(width // 128):
        wide[c] = fine[:, c * 128:(c + 1) * 128].astype(F32)
    groups = []
    for b in range(2):
        picked = jnp.concatenate(
            [wide[c, pl.ds(b, TOK // 2, stride=2), :] for c in range(width // 128)], axis=1
        ).reshape(HALF, 2, HALF, width)
        groups.append((picked[:, 0].reshape(TOK // 4, width), picked[:, 1].reshape(TOK // 4, width)))
    joined = [groups[0][0], groups[0][1], groups[1][0], groups[1][1]]
    count = 4 * width
    mean = sum(jnp.sum(g, axis=-1, keepdims=True) for g in joined) / count
    joined = [g - mean for g in joined]
    spread = sum(jnp.sum(g * g, axis=-1, keepdims=True) for g in joined) / count
    scale = lax.rsqrt(spread + 1e-05)
    ready(4)
    merged = 0.0
    for i, g in enumerate(joined):
        merged = merged + dot((g * scale).astype(BF), vm[i * width:(i + 1) * width, :])
    merged_ref[...] = merged.astype(BF)


def fine_window(i, j, arrays, last, weights, masked, first):
    rows, cols, width = arrays["shape"]
    wide = weights[-1].shape[1]
    blocks = window_blocks(i, j, rows, cols)
    top, left = HALF + i * WIN, HALF + j * WIN
    blocks = [(n, r - top, c - left, *to) if n == "field" else (n, r, c, *to) for n, r, c, *to in blocks]
    arrays = dict(arrays, field=arrays[i, j])
    names = tuple(dict.fromkeys(block[0] for block in blocks))
    flops = 2 * TOK * width * (3 * width + width + 4 * width * 2) + TOK * 2 * width * wide
    size = sum(w.size * 2 for w in weights)
    hbm = pl.BlockSpec(memory_space=pltpu.HBM)
    vmem = pl.BlockSpec(memory_space=pltpu.VMEM)
    held = [jax.ShapeDtypeStruct(w.shape, BF) for w in weights] if first else []
    return pl.pallas_call(
        functools.partial(fine_kernel, masked, first, names, blocks),
        out_shape=[
            jax.ShapeDtypeStruct((TOK, width), BF),
            jax.ShapeDtypeStruct((TOK // 4, wide), BF),
        ]
        + held,
        in_specs=[pl.BlockSpec(memory_space=pltpu.SMEM)] + [vmem] * len(names) + [hbm if first else vmem] * 5,
        out_specs=[vmem] * (2 + len(held)),
        scratch_shapes=[
            pltpu.VMEM((TOK, 3 * width), BF),
            pltpu.VMEM((TOK, width), BF),
            pltpu.VMEM((width // 128, TOK, 128), F32),
            pltpu.VMEM((WIN, WIN, width), BF),
            pltpu.SemaphoreType.DMA((5,)),
        ],
        compiler_params=pltpu.CompilerParams(vmem_limit_bytes=24 << 20),
        cost_estimate=pl.CostEstimate(
            flops=flops, bytes_accessed=size + 3 * TOK * width * 2, transcendentals=TOK * 4 * width * 2
        ),
        name="fine_first" if first else "fine_masked" if masked else "fine_plain",
    )(last, *[arrays[name] for name in names], *weights)


def cut_kernel(parts, offsets, *refs):
    arrays = max(part[0] for part in parts) + 1
    sems = refs[-1]
    copies = []
    for at, (source, out, region, column) in enumerate(parts):
        where = []
        for start, size in region:
            if start is None:
                start = pl.multiple_of(offsets[0], size)
            where.append(pl.ds(start, size))
        src, dst = refs[source].at[tuple(where)], refs[arrays + out]
        if column is not None:
            dst = dst.at[:, pl.ds(column, region[-1][1])]
        copies.append(pltpu.make_async_copy(src, dst, sems.at[at]))
    for copy in copies:
        copy.start()
    for copy in copies:
        copy.wait()


def cut(offsets, arrays, parts, shapes):
    hbm = pl.BlockSpec(memory_space=pltpu.HBM)
    vmem = pl.BlockSpec(memory_space=pltpu.VMEM)
    return pl.pallas_call(
        functools.partial(cut_kernel, tuple(parts)),
        out_shape=[jax.ShapeDtypeStruct(shape, BF) for shape in shapes],
        in_specs=[pl.BlockSpec(memory_space=pltpu.SMEM)] + [hbm] * len(arrays),
        out_specs=[vmem] * len(shapes),
        scratch_shapes=[pltpu.SemaphoreType.DMA((len(parts),))],
        compiler_params=pltpu.CompilerParams(vmem_limit_bytes=8 << 20),
        cost_estimate=pl.CostEstimate(
            flops=0, bytes_accessed=sum(2 * int(np.prod(shape)) for shape in shapes), transcendentals=0
        ),
        name="cut",
    )(offsets, *arrays)


def coarse_kernel(plan, last, table, x_ref, *rest):
    count = max(entry[0] for entry in plan) + 1
    pieces = rest[:count]
    out_ref, xn, qkv, mixed, proj, sem = rest[count:]
    width = x_ref.shape[1]

    def place(slot, rows, columns):
        row = pl.multiple_of(table[2 * slot], rows)
        column = pl.multiple_of(table[2 * slot + 1] * columns, 128)
        return pl.ds(row, rows), pl.ds(column, columns)

    copies, shards = [], {}
    for slot, (piece, r, rows, c, columns, shard, which) in enumerate(plan):
        part = pieces[piece].at[pl.ds(r, rows), pl.ds(c, columns)]
        if which == 1:
            copies.append(pltpu.make_async_copy(part, proj.at[place(slot, rows, columns)], sem.at[len(copies)]))
        else:
            shards.setdefault(shard, []).append((slot, part, rows, columns))
    for copy in copies:
        copy.start()
    xn[...] = norm(x_ref[...].astype(F32))
    for parts in shards.values():
        total = 0.0
        for slot, part, rows, columns in parts:
            row, column = place(slot, rows, columns)
            lhs = xn[...] if rows == width else xn[:, row]
            total = total + dot(lhs, part[...])
        qkv[:, column] = total.astype(BF)
    attention(qkv, mixed, width, mask_bias(last))
    for copy in copies:
        copy.wait()
    step = width // 2
    for at in range(0, width, step):
        cols = slice(at, at + step)
        out_ref[:, cols] = (x_ref[:, cols].astype(F32) + dot(mixed[...], proj[:, cols])).astype(BF)


def coarse_window(x, last, table, pieces, plan):
    width = x.shape[-1]
    vmem = pl.BlockSpec(memory_space=pltpu.VMEM)
    smem = pl.BlockSpec(memory_space=pltpu.SMEM)
    return pl.pallas_call(
        functools.partial(coarse_kernel, plan),
        out_shape=jax.ShapeDtypeStruct((TOK, width), BF),
        in_specs=[smem, smem, vmem] + [vmem] * len(pieces),
        out_specs=vmem,
        scratch_shapes=[
            pltpu.VMEM((TOK, width), BF),
            pltpu.VMEM((TOK, 3 * width), BF),
            pltpu.VMEM((TOK, width), BF),
            pltpu.VMEM((width, width), BF),
            pltpu.SemaphoreType.DMA((sum(entry[6] for entry in plan),)),
        ],
        compiler_params=pltpu.CompilerParams(vmem_limit_bytes=24 << 20),
        cost_estimate=pl.CostEstimate(
            flops=8 * TOK * width * width, bytes_accessed=8 * width * width, transcendentals=TOK * TOK * 16
        ),
        name="coarse",
    )(last, table, x, *pieces)


def line_ring(count):
    return [0] + list(range(1, count, 2)) + list(range(2, count, 2))[::-1]


def moves(order):
    place = {p: i for i, p in enumerate(order)}
    return lambda p, by: order[(place[p] + by) % len(order)]


def send(value, m, n, target):
    pairs = []
    for la in range(m):
        for lo in range(n):
            ta, to = target(la, lo)
            pairs.append((la * n + lo, ta * n + to))
    return lax.ppermute(value, ("lat", "lon"), pairs)


def half_of(ring, la):
    return ring.index(la) % 2


def gather_weights(qkv_shard, proj_shard, part, m, n):
    deep = qkv_shard.shape[0]
    a, b = qkv_shard.shape[1], proj_shard.shape[1]
    half = part.shape[0]
    places = n // 2
    along = moves(line_ring(places))
    ring = line_ring(m)
    across = moves(ring)
    turn = lambda lo: 1 - 2 * (lo % 2)
    origin = lambda lo, s: 2 * along(lo // 2, s) + lo % 2

    def swap(value):
        return send(value, m, n, lambda la, lo: (la, lo ^ 1))

    pieces, plan, spots = [], [], []

    def add(value, spot, rows, key, columns):
        for twin in range(2):
            for c, count, which in columns:
                plan.append((len(pieces), 0, rows, c, count, (twin, key), which))
                spots.append((twin, spot, key))
            pieces.append(swap(value) if twin else value)

    add(qkv_shard, lambda la, lo, key: (0, lo), deep, 0, [(0, a, 0)])
    add(proj_shard, lambda la, lo, key: (0, lo), deep, 0, [(0, b, 1)])
    for s in range(1, places):
        part = send(part, m, n, lambda la, lo: (la, origin(lo, 1)))
        other = send(part, m, n, lambda la, lo: (across(la, turn(lo)), lo))
        for value, flip in ((part, 0), (other, 1)):
            spot = lambda la, lo, key, flip=flip: ((half_of(ring, la) ^ flip) * half, origin(lo, -key))
            add(value, spot, half, s, [(0, a, 0), (a, b, 1)])
    tables = np.zeros((m, n, len(spots), 2), np.int32)
    for la in range(m):
        for lo in range(n):
            tables[la, lo] = [spot(la, lo ^ twin, key) for twin, spot, key in spots]
    table = jnp.asarray(tables.reshape(m * n, -1))[lax.axis_index("lat") * n + lax.axis_index("lon")]
    return pieces, tuple(plan), table


def shifted(value, axis, steps):
    count = lax.axis_size(axis)
    return lax.ppermute(value, axis, [(s, (s + steps) % count) for s in range(count)])


def whole_body(field, qkv_fine, proj_fine, up_fine, down_fine, merge_weight, qkv_coarse, proj_coarse):
    rows, cols, width = field.shape
    wide = merge_weight.shape[1]
    m = lax.axis_size("lat")
    n = lax.axis_size("lon")
    wr, wc = rows // WIN, cols // WIN
    last = (lax.axis_index("lat") == m - 1).astype(jnp.int32).reshape(1)
    fine_weights = (qkv_fine, proj_fine, up_fine, down_fine, merge_weight)

    deep, a = qkv_coarse.shape
    b = proj_coarse.shape[1]
    direct = a % 128 == 0 and b % 128 == 0 and n % 2 == 0 and m % 2 == 0 and deep % (16 * m) == 0
    parts = [
        (0, 0, ((0, rows), (0, HALF), (0, width)), None),
        (0, 1, ((0, HALF), (HALF, cols - HALF), (0, width)), None),
        (0, 2, ((0, HALF), (0, HALF), (0, width)), None),
    ]
    inner = [(i, j) for i in range(wr) for j in range(wc)]
    for at, (i, j) in enumerate(inner):
        top, left = HALF + i * WIN, HALF + j * WIN
        region = ((top, min(WIN, rows - top)), (left, min(WIN, cols - left)), (0, width))
        parts.append((0, 3 + at, region, None))
    shapes = [tuple(size for _, size in part[2]) for part in parts]
    sources = [field]
    lat = lax.axis_index("lat")
    ring = line_ring(m)
    offsets = jnp.asarray(np.array([[half_of(ring, la) * (deep // 2)] for la in range(m)], np.int32))[lat]
    if direct:
        parts.append((1, len(shapes), ((None, deep // 2), (0, a)), 0))
        parts.append((2, len(shapes), ((None, deep // 2), (0, b)), a))
        shapes.append((deep // 2, a + b))
        sources += [qkv_coarse, proj_coarse]
    got = cut(offsets, sources, parts, shapes)
    up = lambda la: (la - 1) % m
    left = lambda lo: (lo - 1) % n
    arrays = {"shape": field.shape}
    for at, place in enumerate(inner):
        arrays[place] = got[3 + at]
    arrays["east"] = send(got[0], m, n, lambda la, lo: (la, left(lo)))
    arrays["south"] = send(got[1], m, n, lambda la, lo: (up(la), lo))
    arrays["corner"] = send(got[2], m, n, lambda la, lo: (up(la), left(lo)))
    if direct:
        pieces, plan, table = gather_weights(qkv_coarse, proj_coarse, got[-1], m, n)
    else:
        pieces = [lax.all_gather(w, "lon", axis=1, tiled=True) for w in (qkv_coarse, proj_coarse)]
        plan = ((0, 0, deep, 0, a * n, 0, 0), (1, 0, deep, 0, b * n, 0, 1))
        table = jnp.zeros((4,), jnp.int32)

    fine, merged = {}, {}
    held = fine_weights
    for i in range(wr):
        for j in range(wc):
            first = i == 0 and j == 0
            out, mer, *kept = fine_window(i, j, arrays, last, held, i == wr - 1, first)
            held = kept if first else held
            fine[i, j] = out.reshape(WIN, WIN, width)
            merged[i, j] = mer.reshape(HALF, HALF, wide)

    def lay(parts):
        return jnp.concatenate(
            [jnp.concatenate([parts[i, j] for j in range(wc)], axis=1) for i in range(wr)], axis=0
        )

    top = jnp.concatenate([merged[0, j][:QUART] for j in range(wc)], axis=1)
    below = shifted(top, "lat", -1)
    side = jnp.concatenate([merged[i, 0][:, :QUART] for i in range(wr)], axis=0)
    side = jnp.concatenate([side[QUART:], below[:, :QUART]], axis=0)
    beside = shifted(side, "lon", -1)
    tall = jnp.concatenate([lay(merged)[QUART:], below], axis=0)
    coarse = jnp.concatenate([tall[:, QUART:], beside], axis=1)

    def back(values):
        down = lambda la: (la + 1) % m
        right = lambda lo: (lo + 1) % n
        side = send(values[:-HALF, -HALF:], m, n, lambda la, lo: (la, right(lo)))
        prev = send(values[-HALF:, :-HALF], m, n, lambda la, lo: (down(la), lo))
        corner = send(values[-HALF:, -HALF:], m, n, lambda la, lo: (down(la), right(lo)))
        top = jnp.concatenate([corner, prev], axis=1)
        return jnp.concatenate([top, jnp.concatenate([side, values[:-HALF, :-HALF]], axis=1)], axis=0)

    fine_out = back(lay(fine))
    cr, cc = rows // 2 // WIN, cols // 2 // WIN
    outs = {}
    for i in range(cr):
        for j in range(cc):
            block = coarse[i * WIN:(i + 1) * WIN, j * WIN:(j + 1) * WIN].reshape(TOK, wide)
            seam = last if i == cr - 1 else jnp.zeros_like(last)
            out = coarse_window(block, seam, table, pieces, plan)
            outs[i, j] = out.reshape(WIN, WIN, wide)
    coarse_out = jnp.concatenate(
        [jnp.concatenate([outs[i, j] for j in range(cc)], axis=1) for i in range(cr)], axis=0
    )
    return fine_out, back(coarse_out)


def solution(mesh):
    in_specs = (P("lat", "lon", None), P(), P(), P(), P(), P(), P(None, "lon"), P(None, "lon"))
    out_specs = (P("lat", "lon", None), P("lat", "lon", None))
    return jax.shard_map(whole_body, mesh=mesh, in_specs=in_specs, out_specs=out_specs, check_vma=False)
```

```python
import functools

import jax
import jax.numpy as jnp
import numpy as np
from jax import lax
from jax.experimental import pallas as pl
from jax.experimental.pallas import tpu as pltpu
from jax.sharding import PartitionSpec as P

HEAD = 64
WIN = 16
HALF = WIN // 2
QUART = HALF // 2
TOK = WIN * WIN
SLAB = 2 * HEAD
NEG = -1e30
BF = jnp.bfloat16
F32 = jnp.float32


def dot(a, b):
    return jnp.dot(a, b, preferred_element_type=F32)


def norm(values):
    center = values - jnp.mean(values, axis=-1, keepdims=True)
    spread = jnp.mean(center * center, axis=-1, keepdims=True)
    return (center * lax.rsqrt(spread + 1e-05)).astype(BF)


def slab_attention(qkv, mixed, at, width, bias):
    q = qkv[:, pl.ds(at, SLAB)] * BF(HEAD ** (-0.5))
    k = qkv[:, pl.ds(at + width, SLAB)]
    v = qkv[:, pl.ds(at + 2 * width, SLAB)]
    low = lax.broadcasted_iota(jnp.int32, (TOK, SLAB), 1) < HEAD
    zero = jnp.zeros_like(q)
    one = jnp.ones_like(v)
    outs = []
    for qh, vh in (
        (jnp.where(low, q, zero), jnp.where(low, v, one)),
        (jnp.where(low, zero, q), jnp.where(low, one, v)),
    ):
        scores = lax.dot_general(qh, k, (((1,), (1,)), ((), ())), preferred_element_type=F32)
        if bias is not None:
            scores = scores + bias
        top = jnp.max(scores, axis=-1, keepdims=True)
        outs.append(dot(jnp.exp(scores - top).astype(BF), vh))
    sums = pltpu.roll(jnp.where(low, outs[1], outs[0]), HEAD, 1)
    mixed[:, pl.ds(at, SLAB)] = (jnp.where(low, outs[0], outs[1]) / sums).astype(BF)


def attention(qkv, mixed, width, bias):
    for at in range(0, width, SLAB):
        slab_attention(qkv, mixed, at, width, bias)


def mask_bias(last_ref):
    lead = lax.broadcasted_iota(jnp.int32, (TOK, TOK), 0) < TOK // 2
    other = lax.broadcasted_iota(jnp.int32, (TOK, TOK), 1) < TOK // 2
    return jnp.where(lead == other, 0.0, jnp.where(last_ref[0] > 0, NEG, 0.0))


def window_blocks(i, j, rows, cols):
    top, left = HALF + i * WIN, HALF + j * WIN
    tall = [(0, top, 0, min(WIN, rows - top))]
    wide = [(0, left, 0, min(WIN, cols - left))]
    if top + WIN > rows:
        tall.append((1, 0, HALF, HALF))
    if left + WIN > cols:
        wide.append((1, 0, HALF, HALF))
    out = []
    for below, r, to_r, count_r in tall:
        for beside, c, to_c, count_c in wide:
            source = ("field", "east", "south", "corner")[2 * below + beside]
            at_c = c - HALF if source == "south" else c
            out.append((source, r, at_c, to_r, to_c, count_r, count_c))
    return out


def fine_kernel(masked, first, names, blocks, last, *refs):
    count = len(names)
    sources = dict(zip(names, refs[:count]))
    weights, refs = refs[count:count + 5], refs[count + 5:]
    out_ref, merged_ref = refs[:2]
    qkv, mixed, wide, window, sems = refs[-5:]
    loads = []
    if first:
        held = refs[2:7]
        for at, (src, dst) in enumerate(zip(weights, held)):
            loads.append(pltpu.make_async_copy(src, dst, sems.at[at]))
            loads[-1].start()
        weights = held
    vq, vp, vu, vd, vm = weights

    def ready(at):
        if first:
            loads[at].wait()

    for name, r, c, to_r, to_c, nr, nc in blocks:
        window[to_r:to_r + nr, to_c:to_c + nc] = sources[name][r:r + nr, c:c + nc]
    width = window.shape[2]
    x = window[...].reshape(TOK, width).astype(F32)
    normed = norm(x)
    ready(0)
    for part in range(3):
        cols = slice(part * width, (part + 1) * width)
        qkv[:, cols] = dot(normed, vq[:, cols]).astype(BF)
    attention(qkv, mixed, width, mask_bias(last) if masked else None)
    ready(1)
    attended = (x + dot(mixed[...], vp[...])).astype(BF).astype(F32)
    normed = norm(attended)
    ready(2)
    ready(3)
    total = attended
    step = width
    for at in range(0, vu.shape[1], step):
        hidden = jax.nn.gelu(dot(normed, vu[:, at:at + step])).astype(BF)
        total = total + dot(hidden, vd[at:at + step, :])
    fine = total.astype(BF)
    out_ref[...] = fine
    for c in range(width // 128):
        wide[c] = fine[:, c * 128:(c + 1) * 128].astype(F32)
    groups = []
    for b in range(2):
        picked = jnp.concatenate(
            [wide[c, pl.ds(b, TOK // 2, stride=2), :] for c in range(width // 128)], axis=1
        ).reshape(HALF, 2, HALF, width)
        groups.append((picked[:, 0].reshape(TOK // 4, width), picked[:, 1].reshape(TOK // 4, width)))
    joined = [groups[0][0], groups[0][1], groups[1][0], groups[1][1]]
    count = 4 * width
    mean = sum(jnp.sum(g, axis=-1, keepdims=True) for g in joined) / count
    joined = [g - mean for g in joined]
    spread = sum(jnp.sum(g * g, axis=-1, keepdims=True) for g in joined) / count
    scale = lax.rsqrt(spread + 1e-05)
    ready(4)
    merged = 0.0
    for i, g in enumerate(joined):
        merged = merged + dot((g * scale).astype(BF), vm[i * width:(i + 1) * width, :])
    merged_ref[...] = merged.astype(BF)


def fine_window(i, j, arrays, last, weights, masked, first):
    rows, cols, width = arrays["shape"]
    wide = weights[-1].shape[1]
    blocks = window_blocks(i, j, rows, cols)
    top, left = HALF + i * WIN, HALF + j * WIN
    blocks = [(n, r - top, c - left, *to) if n == "field" else (n, r, c, *to) for n, r, c, *to in blocks]
    arrays = dict(arrays, field=arrays[i, j])
    names = tuple(dict.fromkeys(block[0] for block in blocks))
    flops = 2 * TOK * width * (3 * width + width + 4 * width * 2) + TOK * 2 * width * wide
    size = sum(w.size * 2 for w in weights)
    hbm = pl.BlockSpec(memory_space=pltpu.HBM)
    vmem = pl.BlockSpec(memory_space=pltpu.VMEM)
    held = [pltpu.VMEM(w.shape, BF) for w in weights] if first else []
    if first:
        weights = [pltpu.with_memory_space_constraint(w, pltpu.HBM) for w in weights]
    return pl.pallas_call(
        functools.partial(fine_kernel, masked, first, names, blocks),
        out_shape=[
            jax.ShapeDtypeStruct((TOK, width), BF),
            jax.ShapeDtypeStruct((TOK // 4, wide), BF),
        ]
        + held,
        in_specs=[pl.BlockSpec(memory_space=pltpu.SMEM)] + [vmem] * len(names) + [hbm if first else vmem] * 5,
        out_specs=[vmem] * (2 + len(held)),
        scratch_shapes=[
            pltpu.VMEM((TOK, 3 * width), BF),
            pltpu.VMEM((TOK, width), BF),
            pltpu.VMEM((width // 128, TOK, 128), F32),
            pltpu.VMEM((WIN, WIN, width), BF),
            pltpu.SemaphoreType.DMA((5,)),
        ],
        compiler_params=pltpu.CompilerParams(vmem_limit_bytes=24 << 20),
        cost_estimate=pl.CostEstimate(
            flops=flops, bytes_accessed=size + 3 * TOK * width * 2, transcendentals=TOK * 4 * width * 2
        ),
        name="fine_first" if first else "fine_masked" if masked else "fine_plain",
    )(last, *[arrays[name] for name in names], *weights)


def cut_kernel(parts, offsets, *refs):
    arrays = max(part[0] for part in parts) + 1
    sems = refs[-1]
    copies = []
    for at, (source, out, region, column) in enumerate(parts):
        where = []
        for start, size in region:
            if start is None:
                start = pl.multiple_of(offsets[0], size)
            where.append(pl.ds(start, size))
        src, dst = refs[source].at[tuple(where)], refs[arrays + out]
        if column is not None:
            dst = dst.at[:, pl.ds(column, region[-1][1])]
        copies.append(pltpu.make_async_copy(src, dst, sems.at[at]))
    for copy in copies:
        copy.start()
    for copy in copies:
        copy.wait()


def cut(offsets, arrays, parts, shapes):
    hbm = pl.BlockSpec(memory_space=pltpu.HBM)
    vmem = pl.BlockSpec(memory_space=pltpu.VMEM)
    return pl.pallas_call(
        functools.partial(cut_kernel, tuple(parts)),
        out_shape=[pltpu.VMEM(shape, BF) for shape in shapes],
        in_specs=[pl.BlockSpec(memory_space=pltpu.SMEM)] + [hbm] * len(arrays),
        out_specs=[vmem] * len(shapes),
        scratch_shapes=[pltpu.SemaphoreType.DMA((len(parts),))],
        compiler_params=pltpu.CompilerParams(vmem_limit_bytes=8 << 20),
        cost_estimate=pl.CostEstimate(
            flops=0, bytes_accessed=sum(2 * int(np.prod(shape)) for shape in shapes), transcendentals=0
        ),
        name="cut",
    )(offsets, *[pltpu.with_memory_space_constraint(array, pltpu.HBM) for array in arrays])


def place(table, slot, rows, columns):
    row = pl.multiple_of(table[2 * slot], rows)
    column = pl.multiple_of(table[2 * slot + 1] * columns, 128)
    return pl.ds(row, rows), pl.ds(column, columns)


def output_copies(plan, table, pieces, proj, sems):
    copies = []
    for slot, piece, r, rows, c, columns, _, which in plan:
        if which == 1:
            part = pieces[piece].at[pl.ds(r, rows), pl.ds(c, columns)]
            at = place(table, slot, rows, columns)
            copies.append(pltpu.make_async_copy(part, proj.at[at], sems.at[len(copies)]))
    return copies


def project_shards(plan, table, pieces, xn, qkv):
    shards = {}
    for slot, piece, r, rows, c, columns, shard, which in plan:
        if which == 0:
            part = pieces[piece].at[pl.ds(r, rows), pl.ds(c, columns)]
            shards.setdefault(shard, []).append((slot, part, rows, columns))
    for parts in shards.values():
        total = 0.0
        for slot, part, rows, columns in parts:
            row, column = place(table, slot, rows, columns)
            lhs = xn[...] if rows == xn.shape[1] else xn[:, row]
            total = total + dot(lhs, part[...])
        qkv[:, column] = total.astype(BF)


def coarse_early_kernel(plan, count, table, x_ref, *rest):
    pieces = rest[:count]
    xn, qkv, proj, sems = rest[count:]
    copies = output_copies(plan, table, pieces, proj, sems)
    for copy in copies:
        copy.start()
    xn[...] = norm(x_ref[...].astype(F32))
    project_shards(plan, table, pieces, xn, qkv)
    for copy in copies:
        copy.wait()


def coarse_late_kernel(plan, count, last, table, x_ref, xn, qkv_in, proj_in, *rest):
    pieces = rest[:count]
    out_ref, qkv, mixed, proj, sems = rest[count:]
    base = pltpu.make_async_copy(proj_in, proj, sems.at[0])
    base.start()
    qkv[...] = qkv_in[...]
    project_shards(plan, table, pieces, xn, qkv)
    base.wait()
    copies = output_copies(plan, table, pieces, proj, sems)
    for copy in copies:
        copy.start()
    width = x_ref.shape[1]
    attention(qkv, mixed, width, mask_bias(last))
    for copy in copies:
        copy.wait()
    step = width // 2
    for at in range(0, width, step):
        cols = slice(at, at + step)
        out_ref[:, cols] = (x_ref[:, cols].astype(F32) + dot(mixed[...], proj[:, cols])).astype(BF)


def split_plan(plan, late):
    chosen = [(slot, entry) for slot, entry in enumerate(plan) if (entry[5][1] in late[1]) == late[0]]
    used = sorted({entry[0] for _, entry in chosen})
    return tuple((slot, used.index(entry[0]), *entry[1:]) for slot, entry in chosen), used


def coarse_window(x, last, table, pieces, plan, late):
    width = x.shape[-1]
    vmem = pl.BlockSpec(memory_space=pltpu.VMEM)
    smem = pl.BlockSpec(memory_space=pltpu.SMEM)
    params = pltpu.CompilerParams(vmem_limit_bytes=24 << 20)

    def cost(share, extra):
        return pl.CostEstimate(
            flops=int(6 * TOK * width * width * share + extra * TOK * width * (2 * width + 4 * TOK)),
            bytes_accessed=int(6 * width * width * share), transcendentals=extra * TOK * TOK * 16)

    early_plan, used = split_plan(plan, (False, late))
    sent = [pieces[k] for k in used]
    xn, qkv, proj = pl.pallas_call(
        functools.partial(coarse_early_kernel, early_plan, len(sent)),
        out_shape=[
            pltpu.VMEM((TOK, width), BF), pltpu.VMEM((TOK, 3 * width), BF), pltpu.VMEM((width, width), BF)
        ],
        in_specs=[smem, vmem] + [vmem] * len(sent),
        out_specs=[vmem] * 3,
        scratch_shapes=[pltpu.SemaphoreType.DMA((len(early_plan),))],
        compiler_params=params,
        cost_estimate=cost(0.75, 0),
        name="coarse_early",
    )(table, x, *sent)
    late_plan, used = split_plan(plan, (True, late))
    sent = [pieces[k] for k in used]
    return pl.pallas_call(
        functools.partial(coarse_late_kernel, late_plan, len(sent)),
        out_shape=jax.ShapeDtypeStruct((TOK, width), BF),
        in_specs=[smem, smem] + [vmem] * (4 + len(sent)),
        out_specs=vmem,
        scratch_shapes=[
            pltpu.VMEM((TOK, 3 * width), BF),
            pltpu.VMEM((TOK, width), BF),
            pltpu.VMEM((width, width), BF),
            pltpu.SemaphoreType.DMA((len(late_plan) + 1,)),
        ],
        compiler_params=params,
        cost_estimate=cost(0.25, 1),
        name="coarse_late",
    )(last, table, x, xn, qkv, proj, *sent)


def line_ring(count):
    return [0] + list(range(1, count, 2)) + list(range(2, count, 2))[::-1]


def moves(order):
    place = {p: i for i, p in enumerate(order)}
    return lambda p, by: order[(place[p] + by) % len(order)]


def send(value, m, n, target):
    pairs = []
    for la in range(m):
        for lo in range(n):
            ta, to = target(la, lo)
            pairs.append((la * n + lo, ta * n + to))
    return lax.ppermute(value, ("lat", "lon"), pairs)


def half_of(ring, la):
    return ring.index(la) % 2


def gather_weights(qkv_shard, proj_shard, part, m, n):
    deep = qkv_shard.shape[0]
    a, b = qkv_shard.shape[1], proj_shard.shape[1]
    half = part.shape[0]
    places = n // 2
    along = moves(line_ring(places))
    ring = line_ring(m)
    across = moves(ring)
    turn = lambda lo: 1 - 2 * (lo % 2)
    origin = lambda lo, s: 2 * along(lo // 2, s) + lo % 2

    def swap(value):
        return send(value, m, n, lambda la, lo: (la, lo ^ 1))

    pieces, plan, spots = [], [], []

    def add(value, spot, rows, key, columns):
        for twin in range(2):
            for c, count, which in columns:
                plan.append((len(pieces), 0, rows, c, count, (twin, key), which))
                spots.append((twin, spot, key))
            pieces.append(swap(value) if twin else value)

    add(qkv_shard, lambda la, lo, key: (0, lo), deep, 0, [(0, a, 0)])
    add(proj_shard, lambda la, lo, key: (0, lo), deep, 0, [(0, b, 1)])
    for s in range(1, places):
        part = send(part, m, n, lambda la, lo: (la, origin(lo, 1)))
        other = send(part, m, n, lambda la, lo: (across(la, turn(lo)), lo))
        for value, flip in ((part, 0), (other, 1)):
            spot = lambda la, lo, key, flip=flip: ((half_of(ring, la) ^ flip) * half, origin(lo, -key))
            add(value, spot, half, s, [(0, a, 0), (a, b, 1)])
    tables = np.zeros((m, n, len(spots), 2), np.int32)
    for la in range(m):
        for lo in range(n):
            tables[la, lo] = [spot(la, lo ^ twin, key) for twin, spot, key in spots]
    table = jnp.asarray(tables.reshape(m * n, -1))[lax.axis_index("lat") * n + lax.axis_index("lon")]
    return pieces, tuple(plan), table


def shifted(value, axis, steps):
    count = lax.axis_size(axis)
    return lax.ppermute(value, axis, [(s, (s + steps) % count) for s in range(count)])


def whole_body(field, qkv_fine, proj_fine, up_fine, down_fine, merge_weight, qkv_coarse, proj_coarse):
    rows, cols, width = field.shape
    wide = merge_weight.shape[1]
    m = lax.axis_size("lat")
    n = lax.axis_size("lon")
    wr, wc = rows // WIN, cols // WIN
    last = (lax.axis_index("lat") == m - 1).astype(jnp.int32).reshape(1)
    fine_weights = (qkv_fine, proj_fine, up_fine, down_fine, merge_weight)

    deep, a = qkv_coarse.shape
    b = proj_coarse.shape[1]
    direct = a % 128 == 0 and b % 128 == 0 and n % 2 == 0 and m % 2 == 0 and deep % (16 * m) == 0
    parts = [
        (0, 0, ((0, rows), (0, HALF), (0, width)), None),
        (0, 1, ((0, HALF), (HALF, cols - HALF), (0, width)), None),
        (0, 2, ((0, HALF), (0, HALF), (0, width)), None),
    ]
    inner = [(i, j) for i in range(wr) for j in range(wc)]
    for at, (i, j) in enumerate(inner):
        top, left = HALF + i * WIN, HALF + j * WIN
        region = ((top, min(WIN, rows - top)), (left, min(WIN, cols - left)), (0, width))
        parts.append((0, 3 + at, region, None))
    shapes = [tuple(size for _, size in part[2]) for part in parts]
    sources = [field]
    lat = lax.axis_index("lat")
    ring = line_ring(m)
    offsets = jnp.asarray(np.array([[half_of(ring, la) * (deep // 2)] for la in range(m)], np.int32))[lat]
    if direct:
        parts.append((1, len(shapes), ((None, deep // 2), (0, a)), 0))
        parts.append((2, len(shapes), ((None, deep // 2), (0, b)), a))
        shapes.append((deep // 2, a + b))
        sources += [qkv_coarse, proj_coarse]
    got = cut(offsets, sources, parts, shapes)
    up = lambda la: (la - 1) % m
    left = lambda lo: (lo - 1) % n
    arrays = {"shape": field.shape}
    for at, place in enumerate(inner):
        arrays[place] = got[3 + at]
    arrays["east"] = send(got[0], m, n, lambda la, lo: (la, left(lo)))
    arrays["south"] = send(got[1], m, n, lambda la, lo: (up(la), lo))
    arrays["corner"] = send(got[2], m, n, lambda la, lo: (up(la), left(lo)))
    if direct:
        pieces, plan, table = gather_weights(qkv_coarse, proj_coarse, got[-1], m, n)
    else:
        pieces = [lax.all_gather(w, "lon", axis=1, tiled=True) for w in (qkv_coarse, proj_coarse)]
        plan = ((0, 0, deep, 0, a * n, (0, 0), 0), (1, 0, deep, 0, b * n, (0, 0), 1))
        table = jnp.zeros((4,), jnp.int32)

    fine, merged = {}, {}
    held = fine_weights
    for i in range(wr):
        for j in range(wc):
            first = i == 0 and j == 0
            out, mer, *kept = fine_window(i, j, arrays, last, held, i == wr - 1, first)
            held = kept if first else held
            fine[i, j] = out.reshape(WIN, WIN, width)
            merged[i, j] = mer.reshape(HALF, HALF, wide)

    def lay(parts):
        return jnp.concatenate(
            [jnp.concatenate([parts[i, j] for j in range(wc)], axis=1) for i in range(wr)], axis=0
        )

    top = jnp.concatenate([merged[0, j][:QUART] for j in range(wc)], axis=1)
    below = shifted(top, "lat", -1)
    side = jnp.concatenate([merged[i, 0][:, :QUART] for i in range(wr)], axis=0)
    side = jnp.concatenate([side[QUART:], below[:, :QUART]], axis=0)
    beside = shifted(side, "lon", -1)
    tall = jnp.concatenate([lay(merged)[QUART:], below], axis=0)
    coarse = jnp.concatenate([tall[:, QUART:], beside], axis=1)

    def back(values):
        down = lambda la: (la + 1) % m
        right = lambda lo: (lo + 1) % n
        side = send(values[:-HALF, -HALF:], m, n, lambda la, lo: (la, right(lo)))
        prev = send(values[-HALF:, :-HALF], m, n, lambda la, lo: (down(la), lo))
        corner = send(values[-HALF:, -HALF:], m, n, lambda la, lo: (down(la), right(lo)))
        top = jnp.concatenate([corner, prev], axis=1)
        return jnp.concatenate([top, jnp.concatenate([side, values[:-HALF, :-HALF]], axis=1)], axis=0)

    fine_out = back(lay(fine))
    cr, cc = rows // 2 // WIN, cols // 2 // WIN
    outs = {}
    for i in range(cr):
        for j in range(cc):
            block = coarse[i * WIN:(i + 1) * WIN, j * WIN:(j + 1) * WIN].reshape(TOK, wide)
            seam = last if i == cr - 1 else jnp.zeros_like(last)
            out = coarse_window(block, seam, table, pieces, plan, (n // 2 - 1,) if direct else ())
            outs[i, j] = out.reshape(WIN, WIN, wide)
    coarse_out = jnp.concatenate(
        [jnp.concatenate([outs[i, j] for j in range(cc)], axis=1) for i in range(cr)], axis=0
    )
    return fine_out, back(coarse_out)


def solution(mesh):
    in_specs = (P("lat", "lon", None), P(), P(), P(), P(), P(), P(None, "lon"), P(None, "lon"))
    out_specs = (P("lat", "lon", None), P("lat", "lon", None))
    return jax.shard_map(whole_body, mesh=mesh, in_specs=in_specs, out_specs=out_specs, check_vma=False)
```

```python
import functools

import jax
import jax.numpy as jnp
import numpy as np
from jax import lax
from jax.experimental import pallas as pl
from jax.experimental.pallas import tpu as pltpu
from jax.sharding import PartitionSpec as P

HEAD = 64
WIN = 16
HALF = WIN // 2
QUART = HALF // 2
TOK = WIN * WIN
SLAB = 2 * HEAD
NEG = -1e30
BF = jnp.bfloat16
F32 = jnp.float32


def dot(a, b):
    return jnp.dot(a, b, preferred_element_type=F32)


def norm(values):
    center = values - jnp.mean(values, axis=-1, keepdims=True)
    spread = jnp.mean(center * center, axis=-1, keepdims=True)
    return (center * lax.rsqrt(spread + 1e-05)).astype(BF)


def slab_attention(qkv, mixed, at, width, bias):
    q = qkv[:, pl.ds(at, SLAB)] * BF(HEAD ** (-0.5))
    k = qkv[:, pl.ds(at + width, SLAB)]
    v = qkv[:, pl.ds(at + 2 * width, SLAB)]
    low = lax.broadcasted_iota(jnp.int32, (TOK, SLAB), 1) < HEAD
    zero = jnp.zeros_like(q)
    one = jnp.ones_like(v)
    outs = []
    for qh, vh in (
        (jnp.where(low, q, zero), jnp.where(low, v, one)),
        (jnp.where(low, zero, q), jnp.where(low, one, v)),
    ):
        scores = lax.dot_general(qh, k, (((1,), (1,)), ((), ())), preferred_element_type=F32)
        if bias is not None:
            scores = scores + bias
        top = jnp.max(scores, axis=-1, keepdims=True)
        outs.append(dot(jnp.exp(scores - top).astype(BF), vh))
    sums = pltpu.roll(jnp.where(low, outs[1], outs[0]), HEAD, 1)
    mixed[:, pl.ds(at, SLAB)] = (jnp.where(low, outs[0], outs[1]) / sums).astype(BF)


def attention(qkv, mixed, width, bias):
    for at in range(0, width, SLAB):
        slab_attention(qkv, mixed, at, width, bias)


def mask_bias(here, seam):
    lead = lax.broadcasted_iota(jnp.int32, (TOK, TOK), 0) < TOK // 2
    other = lax.broadcasted_iota(jnp.int32, (TOK, TOK), 1) < TOK // 2
    return jnp.where(lead == other, 0.0, jnp.where(here[0] == seam, NEG, 0.0))


def window_blocks(i, j, rows, cols):
    top, left = HALF + i * WIN, HALF + j * WIN
    tall = [(0, top, 0, min(WIN, rows - top))]
    wide = [(0, left, 0, min(WIN, cols - left))]
    if top + WIN > rows:
        tall.append((1, 0, HALF, HALF))
    if left + WIN > cols:
        wide.append((1, 0, HALF, HALF))
    out = []
    for below, r, to_r, count_r in tall:
        for beside, c, to_c, count_c in wide:
            source = ("field", "east", "south", "corner")[2 * below + beside]
            at_c = c - HALF if source == "south" else c
            out.append((source, r, at_c, to_r, to_c, count_r, count_c))
    return out


def fine_kernel(masked, first, names, blocks, wr, wc, ends, last, *refs):
    count = len(names)
    sources = dict(zip(names, refs[:count]))
    weights, refs = refs[count:count + 5], refs[count + 5:]
    edges, refs = refs[:ends], refs[ends:]
    out_ref, merged_ref = refs[:2]
    qkv, mixed, wide, window, sems = refs[-5:]
    loads = []
    if first:
        held = refs[2:7]
        for at, (src, dst) in enumerate(zip(weights, held)):
            loads.append(pltpu.make_async_copy(src, dst, sems.at[at]))
            loads[-1].start()
        weights = held
    vq, vp, vu, vd, vm = weights

    def ready(at):
        if first:
            loads[at].wait()

    for name, r, c, to_r, to_c, nr, nc in blocks:
        window[to_r:to_r + nr, to_c:to_c + nc] = sources[name][r:r + nr, c:c + nc]
    width = window.shape[2]
    x = window[...].reshape(TOK, width).astype(F32)
    normed = norm(x)
    ready(0)
    for part in range(3):
        cols = slice(part * width, (part + 1) * width)
        qkv[:, cols] = dot(normed, vq[:, cols]).astype(BF)
    attention(qkv, mixed, width, mask_bias(last, masked) if masked is not None else None)
    ready(1)
    attended = (x + dot(mixed[...], vp[...])).astype(BF).astype(F32)
    normed = norm(attended)
    ready(2)
    ready(3)
    total = attended
    step = width
    for at in range(0, vu.shape[1], step):
        hidden = jax.nn.gelu(dot(normed, vu[:, at:at + step])).astype(BF)
        total = total + dot(hidden, vd[at:at + step, :])
    fine = total.astype(BF)
    out_ref[...] = fine
    if ends:
        own = fine.reshape(WIN, WIN, width)
        to_e, to_s, to_d = refs[2:5]
        for at in range(wr - 1):
            to_e[at * WIN:(at + 1) * WIN] = edges[at][:, HALF:]
        to_e[(wr - 1) * WIN:] = own[:HALF, HALF:]
        for at in range(wc - 1):
            to_s[:, at * WIN:(at + 1) * WIN] = edges[wr - 1 + at][HALF:]
        to_s[:, (wc - 1) * WIN:] = own[HALF:, :HALF]
        to_d[...] = own[HALF:, HALF:]
    for c in range(width // 128):
        wide[c] = fine[:, c * 128:(c + 1) * 128].astype(F32)
    groups = []
    for b in range(2):
        picked = jnp.concatenate(
            [wide[c, pl.ds(b, TOK // 2, stride=2), :] for c in range(width // 128)], axis=1
        ).reshape(HALF, 2, HALF, width)
        groups.append((picked[:, 0].reshape(TOK // 4, width), picked[:, 1].reshape(TOK // 4, width)))
    joined = [groups[0][0], groups[0][1], groups[1][0], groups[1][1]]
    count = 4 * width
    mean = sum(jnp.sum(g, axis=-1, keepdims=True) for g in joined) / count
    joined = [g - mean for g in joined]
    spread = sum(jnp.sum(g * g, axis=-1, keepdims=True) for g in joined) / count
    scale = lax.rsqrt(spread + 1e-05)
    ready(4)
    merged = 0.0
    for i, g in enumerate(joined):
        merged = merged + dot((g * scale).astype(BF), vm[i * width:(i + 1) * width, :])
    merged_ref[...] = merged.astype(BF)


def fine_window(i, j, arrays, last, weights, masked, first, edges=None):
    rows, cols, width = arrays["shape"]
    wide = weights[-1].shape[1]
    blocks = window_blocks(i, j, rows, cols)
    top, left = HALF + i * WIN, HALF + j * WIN
    blocks = [(n, r - top, c - left, *to) if n == "field" else (n, r, c, *to) for n, r, c, *to in blocks]
    arrays = dict(arrays, field=arrays[i, j])
    names = tuple(dict.fromkeys(block[0] for block in blocks))
    flops = 2 * TOK * width * (3 * width + width + 4 * width * 2) + TOK * 2 * width * wide
    size = sum(w.size * 2 for w in weights)
    wr, wc = rows // WIN, cols // WIN
    edges = edges or []
    sends = []
    if edges:
        sends = [(rows - HALF, HALF, width), (HALF, cols - HALF, width), (HALF, HALF, width)]
    hbm = pl.BlockSpec(memory_space=pltpu.HBM)
    vmem = pl.BlockSpec(memory_space=pltpu.VMEM)
    held = [pltpu.VMEM(w.shape, BF) for w in weights] if first else []
    if first:
        weights = [pltpu.with_memory_space_constraint(w, pltpu.HBM) for w in weights]
    return pl.pallas_call(
        functools.partial(fine_kernel, masked, first, names, blocks, wr, wc, len(edges)),
        out_shape=[
            jax.ShapeDtypeStruct((TOK, width), BF),
            jax.ShapeDtypeStruct((TOK // 4, wide), BF),
        ]
        + held
        + [pltpu.VMEM(shape, BF) for shape in sends],
        in_specs=[pl.BlockSpec(memory_space=pltpu.SMEM)] + [vmem] * len(names) + [hbm if first else vmem] * 5 + [vmem] * len(edges),
        out_specs=[vmem] * (2 + len(held) + len(sends)),
        scratch_shapes=[
            pltpu.VMEM((TOK, 3 * width), BF),
            pltpu.VMEM((TOK, width), BF),
            pltpu.VMEM((width // 128, TOK, 128), F32),
            pltpu.VMEM((WIN, WIN, width), BF),
            pltpu.SemaphoreType.DMA((5,)),
        ],
        compiler_params=pltpu.CompilerParams(vmem_limit_bytes=14 << 20),
        cost_estimate=pl.CostEstimate(
            flops=flops, bytes_accessed=size + 3 * TOK * width * 2, transcendentals=TOK * 4 * width * 2
        ),
        name="fine_first" if first else "fine_masked" if masked is not None else "fine_plain",
    )(last, *[arrays[name] for name in names], *weights, *edges)


def cut_kernel(parts, starts, here, *refs):
    arrays = max(part[0] for part in parts) + 1
    sems = refs[-1]
    copies = []
    for at, (source, out, region, column) in enumerate(parts):
        where = []
        for start, size in region:
            if start is None:
                start = pl.multiple_of(pick(here[0], starts), size)
            where.append(pl.ds(start, size))
        src, dst = refs[source].at[tuple(where)], refs[arrays + out]
        if column is not None:
            dst = dst.at[:, pl.ds(column, region[-1][1])]
        copies.append(pltpu.make_async_copy(src, dst, sems.at[at]))
    for copy in copies:
        copy.start()
    for copy in copies:
        copy.wait()


def cut(here, starts, arrays, parts, shapes):
    hbm = pl.BlockSpec(memory_space=pltpu.HBM)
    vmem = pl.BlockSpec(memory_space=pltpu.VMEM)
    return pl.pallas_call(
        functools.partial(cut_kernel, tuple(parts), starts),
        out_shape=[pltpu.VMEM(shape, BF) for shape in shapes],
        in_specs=[pl.BlockSpec(memory_space=pltpu.SMEM)] + [hbm] * len(arrays),
        out_specs=[vmem] * len(shapes),
        scratch_shapes=[pltpu.SemaphoreType.DMA((len(parts),))],
        compiler_params=pltpu.CompilerParams(vmem_limit_bytes=8 << 20),
        cost_estimate=pl.CostEstimate(
            flops=0, bytes_accessed=sum(2 * int(np.prod(shape)) for shape in shapes), transcendentals=0
        ),
        name="cut",
    )(here, *[pltpu.with_memory_space_constraint(array, pltpu.HBM) for array in arrays])


def pick(index, values):
    out = jnp.int32(values[0])
    for at in range(1, len(values)):
        out = jnp.where(index == at, jnp.int32(values[at]), out)
    return out


def place(here, spot, rows, columns):
    row = pl.multiple_of(pick(here[0], spot[0]), rows)
    column = pl.multiple_of(pick(here[1], spot[1]) * columns, 128)
    return pl.ds(row, rows), pl.ds(column, columns)


def output_copies(plan, here, pieces, proj, sems):
    copies = []
    for piece, r, rows, c, columns, _, which, spot in plan:
        if which == 1:
            part = pieces[piece].at[pl.ds(r, rows), pl.ds(c, columns)]
            at = place(here, spot, rows, columns)
            copies.append(pltpu.make_async_copy(part, proj.at[at], sems.at[len(copies)]))
    return copies


def project_shards(plan, here, pieces, xn, qkv):
    shards = {}
    for piece, r, rows, c, columns, shard, which, spot in plan:
        if which == 0:
            part = pieces[piece].at[pl.ds(r, rows), pl.ds(c, columns)]
            shards.setdefault(shard, []).append((spot, part, rows, columns))
    for parts in shards.values():
        total = 0.0
        for spot, part, rows, columns in parts:
            row, column = place(here, spot, rows, columns)
            lhs = xn[...] if rows == xn.shape[1] else xn[:, row]
            total = total + dot(lhs, part[...])
        qkv[:, column] = total.astype(BF)


def coarse_early_kernel(plan, count, blocks, here, *rest):
    pieces, rest = rest[:count], rest[count:]
    x, xn, qkv, proj, window, sems = rest[-6:]
    copies = output_copies(plan, here, pieces, proj, sems)
    for copy in copies:
        copy.start()
    for source, r, c, to_r, to_c, nr, nc in blocks:
        window[to_r:to_r + nr, to_c:to_c + nc] = rest[source][r:r + nr, c:c + nc]
    value = window[...].reshape(x.shape)
    x[...] = value
    xn[...] = norm(value.astype(F32))
    project_shards(plan, here, pieces, xn, qkv)
    for copy in copies:
        copy.wait()


def coarse_late_kernel(plan, count, seam, here, x_ref, xn, qkv_in, proj_in, *rest):
    pieces = rest[:count]
    out_ref, qkv, mixed, proj, sems = rest[count:]
    base = pltpu.make_async_copy(proj_in, proj, sems.at[0])
    base.start()
    qkv[...] = qkv_in[...]
    project_shards(plan, here, pieces, xn, qkv)
    base.wait()
    copies = output_copies(plan, here, pieces, proj, sems)
    for copy in copies:
        copy.start()
    width = x_ref.shape[1]
    attention(qkv, mixed, width, mask_bias(here, seam) if seam is not None else None)
    for copy in copies:
        copy.wait()
    step = width // 2
    for at in range(0, width, step):
        cols = slice(at, at + step)
        out_ref[:, cols] = (x_ref[:, cols].astype(F32) + dot(mixed[...], proj[:, cols])).astype(BF)


def split_plan(plan, late):
    chosen = [entry for entry in plan if (entry[5][1] in late[1]) == late[0]]
    used = sorted({entry[0] for entry in chosen})
    return tuple((used.index(entry[0]), *entry[1:]) for entry in chosen), used


def coarse_window(arrays, blocks, seam, here, pieces, plan, late):
    width = arrays[0].shape[-1]
    vmem = pl.BlockSpec(memory_space=pltpu.VMEM)
    smem = pl.BlockSpec(memory_space=pltpu.SMEM)
    params = pltpu.CompilerParams(vmem_limit_bytes=14 << 20)

    def cost(share, extra):
        return pl.CostEstimate(
            flops=int(6 * TOK * width * width * share + extra * TOK * width * (2 * width + 4 * TOK)),
            bytes_accessed=int(6 * width * width * share), transcendentals=extra * TOK * TOK * 16)

    early_plan, used = split_plan(plan, (False, late))
    sent = [pieces[k] for k in used]
    x, xn, qkv, proj = pl.pallas_call(
        functools.partial(coarse_early_kernel, early_plan, len(sent), blocks),
        out_shape=[
            pltpu.VMEM((TOK, width), BF), pltpu.VMEM((TOK, width), BF), pltpu.VMEM((TOK, 3 * width), BF), pltpu.VMEM((width, width), BF)
        ],
        in_specs=[smem] + [vmem] * (len(sent) + len(arrays)),
        out_specs=[vmem] * 4,
        scratch_shapes=[pltpu.VMEM((WIN, WIN, width), BF), pltpu.SemaphoreType.DMA((len(early_plan),))],
        compiler_params=params,
        cost_estimate=cost(0.75, 0),
        name="coarse_early",
    )(here, *sent, *arrays)
    late_plan, used = split_plan(plan, (True, late))
    sent = [pieces[k] for k in used]
    return pl.pallas_call(
        functools.partial(coarse_late_kernel, late_plan, len(sent), seam),
        out_shape=jax.ShapeDtypeStruct((TOK, width), BF),
        in_specs=[smem] + [vmem] * (4 + len(sent)),
        out_specs=vmem,
        scratch_shapes=[
            pltpu.VMEM((TOK, 3 * width), BF),
            pltpu.VMEM((TOK, width), BF),
            pltpu.VMEM((width, width), BF),
            pltpu.SemaphoreType.DMA((len(late_plan) + 1,)),
        ],
        compiler_params=params,
        cost_estimate=cost(0.25, 1),
        name="coarse_late",
    )(here, x, xn, qkv, proj, *sent)


def coarse_blocks(i, j, wr, wc):
    def segments(start):
        out, at = [], start
        while at < start + WIN:
            size = min(HALF - at % HALF, start + WIN - at)
            out.append((at // HALF, at % HALF, at - start, size))
            at += size
        return out

    blocks = []
    for p, r, to_r, nr in segments(QUART + i * WIN):
        for q, c, to_c, nc in segments(QUART + j * WIN):
            if q == wc:
                blocks.append((wr * wc + 1, i * WIN + to_r, 0, to_r, to_c, nr, nc))
            elif p == wr:
                blocks.append((wr * wc, 0, q * HALF + c, to_r, to_c, nr, nc))
            else:
                blocks.append((p * wc + q, r, c, to_r, to_c, nr, nc))
    return tuple(blocks)


def line_ring(count):
    return [0] + list(range(1, count, 2)) + list(range(2, count, 2))[::-1]


def moves(order):
    place = {p: i for i, p in enumerate(order)}
    return lambda p, by: order[(place[p] + by) % len(order)]


def send(value, m, n, target):
    pairs = []
    for la in range(m):
        for lo in range(n):
            ta, to = target(la, lo)
            pairs.append((la * n + lo, ta * n + to))
    return lax.ppermute(value, ("lat", "lon"), pairs)


def half_of(ring, la):
    return ring.index(la) % 2


def gather_weights(qkv_shard, proj_shard, part, m, n):
    deep = qkv_shard.shape[0]
    a, b = qkv_shard.shape[1], proj_shard.shape[1]
    half = part.shape[0]
    places = n // 2
    along = moves(line_ring(places))
    ring = line_ring(m)
    across = moves(ring)
    turn = lambda lo: 1 - 2 * (lo % 2)
    origin = lambda lo, s: 2 * along(lo // 2, s) + lo % 2

    def swap(value):
        return send(value, m, n, lambda la, lo: (la, lo ^ 1))

    pieces, plan = [], []

    def add(value, by_lat, rows, key, columns):
        for twin in range(2):
            for c, count, which in columns:
                spot = (by_lat, tuple(origin(lo ^ twin, -key) for lo in range(n)))
                plan.append((len(pieces), 0, rows, c, count, (twin, key), which, spot))
            pieces.append(swap(value) if twin else value)

    add(qkv_shard, (0,) * m, deep, 0, [(0, a, 0)])
    add(proj_shard, (0,) * m, deep, 0, [(0, b, 1)])
    for s in range(1, places):
        part = send(part, m, n, lambda la, lo: (la, origin(lo, 1)))
        other = send(part, m, n, lambda la, lo: (across(la, turn(lo)), lo))
        for value, flip in ((part, 0), (other, 1)):
            by_lat = tuple((half_of(ring, la) ^ flip) * half for la in range(m))
            add(value, by_lat, half, s, [(0, a, 0), (a, b, 1)])
    return pieces, tuple(plan)


def shifted(value, axis, steps):
    count = lax.axis_size(axis)
    return lax.ppermute(value, axis, [(s, (s + steps) % count) for s in range(count)])


def whole_body(field, qkv_fine, proj_fine, up_fine, down_fine, merge_weight, qkv_coarse, proj_coarse):
    rows, cols, width = field.shape
    wide = merge_weight.shape[1]
    m = lax.axis_size("lat")
    n = lax.axis_size("lon")
    wr, wc = rows // WIN, cols // WIN
    here = jnp.stack([lax.axis_index("lat"), lax.axis_index("lon")]).astype(jnp.int32)
    fine_weights = (qkv_fine, proj_fine, up_fine, down_fine, merge_weight)

    deep, a = qkv_coarse.shape
    b = proj_coarse.shape[1]
    direct = a % 128 == 0 and b % 128 == 0 and n % 2 == 0 and m % 2 == 0 and deep % (16 * m) == 0
    parts = [
        (0, 0, ((0, rows), (0, HALF), (0, width)), None),
        (0, 1, ((0, HALF), (HALF, cols - HALF), (0, width)), None),
        (0, 2, ((0, HALF), (0, HALF), (0, width)), None),
    ]
    inner = [(i, j) for i in range(wr) for j in range(wc)]
    for at, (i, j) in enumerate(inner):
        top, left = HALF + i * WIN, HALF + j * WIN
        region = ((top, min(WIN, rows - top)), (left, min(WIN, cols - left)), (0, width))
        parts.append((0, 3 + at, region, None))
    shapes = [tuple(size for _, size in part[2]) for part in parts]
    sources = [field]
    ring = line_ring(m)
    starts = tuple(half_of(ring, la) * (deep // 2) for la in range(m))
    if direct:
        parts.append((1, len(shapes), ((None, deep // 2), (0, a)), 0))
        parts.append((2, len(shapes), ((None, deep // 2), (0, b)), a))
        shapes.append((deep // 2, a + b))
        sources += [qkv_coarse, proj_coarse]
    got = cut(here, starts, sources, parts, shapes)
    up = lambda la: (la - 1) % m
    left = lambda lo: (lo - 1) % n
    arrays = {"shape": field.shape}
    for at, place in enumerate(inner):
        arrays[place] = got[3 + at]
    arrays["east"] = send(got[0], m, n, lambda la, lo: (la, left(lo)))
    arrays["south"] = send(got[1], m, n, lambda la, lo: (up(la), lo))
    arrays["corner"] = send(got[2], m, n, lambda la, lo: (up(la), left(lo)))
    if direct:
        pieces, plan = gather_weights(qkv_coarse, proj_coarse, got[-1], m, n)
    else:
        pieces = [lax.all_gather(w, "lon", axis=1, tiled=True) for w in (qkv_coarse, proj_coarse)]
        plan = ((0, 0, deep, 0, a * n, (0, 0), 0, ((0,), (0,))), (1, 0, deep, 0, b * n, (0, 0), 1, ((0,), (0,))))

    fine, merged = {}, {}
    held = fine_weights
    for i in range(wr):
        for j in range(wc):
            first = i == 0 and j == 0
            edges = None
            if wr * wc > 1 and (i, j) == (wr - 1, wc - 1):
                edges = [fine[p, wc - 1] for p in range(wr - 1)] + [fine[wr - 1, q] for q in range(wc - 1)]
            out, mer, *more = fine_window(
                i, j, arrays, here, held, m - 1 if i == wr - 1 else None, first, edges)
            held = more[:5] if first else held
            sends = more if edges else None
            fine[i, j] = out.reshape(WIN, WIN, width)
            merged[i, j] = mer.reshape(HALF, HALF, wide)

    def lay(parts):
        return jnp.concatenate(
            [jnp.concatenate([parts[i, j] for j in range(wc)], axis=1) for i in range(wr)], axis=0
        )

    top = jnp.concatenate([merged[0, j][:QUART] for j in range(wc)], axis=1)
    below = shifted(top, "lat", -1)
    side = jnp.concatenate([merged[i, 0][:, :QUART] for i in range(wr)], axis=0)
    side = jnp.concatenate([side[QUART:], below[:, :QUART]], axis=0)
    beside = shifted(side, "lon", -1)

    def back(values, sends=None):
        down = lambda la: (la + 1) % m
        right = lambda lo: (lo + 1) % n
        sends = sends or (values[:-HALF, -HALF:], values[-HALF:, :-HALF], values[-HALF:, -HALF:])
        side = send(sends[0], m, n, lambda la, lo: (la, right(lo)))
        prev = send(sends[1], m, n, lambda la, lo: (down(la), lo))
        corner = send(sends[2], m, n, lambda la, lo: (down(la), right(lo)))
        top = jnp.concatenate([corner, prev], axis=1)
        return jnp.concatenate([top, jnp.concatenate([side, values[:-HALF, :-HALF]], axis=1)], axis=0)

    fine_out = back(lay(fine), sends)
    cr, cc = rows // 2 // WIN, cols // 2 // WIN
    outs = {}
    for i in range(cr):
        for j in range(cc):
            tiles = [merged[p, q] for p in range(wr) for q in range(wc)] + [below, beside]
            out = coarse_window(
                tiles, coarse_blocks(i, j, wr, wc), m - 1 if i == cr - 1 else None, here, pieces, plan,
                (n // 2 - 1,) if direct else ())
            outs[i, j] = out.reshape(WIN, WIN, wide)
    coarse_out = jnp.concatenate(
        [jnp.concatenate([outs[i, j] for j in range(cc)], axis=1) for i in range(cr)], axis=0
    )
    return fine_out, back(coarse_out)


def solution(mesh):
    in_specs = (P("lat", "lon", None), P(), P(), P(), P(), P(), P(None, "lon"), P(None, "lon"))
    out_specs = (P("lat", "lon", None), P("lat", "lon", None))
    return jax.shard_map(whole_body, mesh=mesh, in_specs=in_specs, out_specs=out_specs, check_vma=False)
```
